128 devices in a mesh: gx: 8 (over y, core), gy: 16 (over z, x).
Axes of the slice: x: 4, y: 4, z: 4, core: 2. Of those that a mesh axis runs over, the one named last changes fastest.
Arguments:
- positions: float32 [3, 2097152], P(None, ('gx', 'gy')), may hold values from 0 to 128, as said below
- point_feat: float32 [32, 2097152], P(None, ('gx', 'gy')), may hold values from -1.8 to 1.8
- area: float32 [2097152], P(('gx', 'gy')), may hold values from 0.3 to 3
- block_brick: int32 [16384], P(('gx', 'gy')), may hold values from 0 to 4095, as said below
- block_count: int32 [128], P(('gx', 'gy')), may hold values from 8 to 128, as said below
- sdf: float32 [128, 128, 128], P('gx', 'gy'), may hold values from -6 to 6
- grid_gain: float32 [32], replicated, may hold values from -4 to 4
- mix_w: float32 [2, 32, 32], replicated, may hold values from -1 to 1
- mix_b: float32 [2, 32], replicated, may hold values from -1.8 to 1.8
- spec_w: float32 [2, 2, 16, 32, 1024], P(None, None, 'gy', 'gx'), may hold values from -18 to 18
- readout_w: float32 [32], replicated, may hold values from -1 to 1
Outputs:
- pressure: float32 [2097152], P(('gx', 'gy'))
The draws below stay inside these ranges and needn't reach their ends.
Inputs may be any that keep to these rules, and one draw needn't show every extreme that they name: `block_brick`: block n belongs to partition d = n // 128. Its brick b lies in the grid pencil row of that partition: (b // 256) // 2 == d // 16. Of the blocks of one partition at most 8 lie in the bricks of one pencil, the pencil of b being ((b // 16) % 16); in every pencil row some pencil holds exactly 8 of the first 8 blocks of every partition of that row. The live blocks of partition d are its first block_count[d] blocks; some partition has all 128 live and some has exactly 8. `positions`: every point lies inside its block's brick, 0.5 or more from each of the brick's faces.
All inputs are finite; a program needn't handle non-finite values.
Results may differ from the reference program's by a relative error of at most 0.0003.
Values sent between devices are 32-bit elements; how exact they have to be, the bound alone decides.
A program may use at most 128 MiB of HBM per device.

```python
import math
import jax
import jax.numpy as jnp
from jax import lax

G = 128
C = 32
M = 32
B = 8
PB = 128
LAYERS = 2
BLK_DEV = 128
KZ = 16
NB = 16
NBX = 2
NBY = 1
CAP = 8
PARTITIONS = 128
NBLK = 16384
NPTS = 2097152


def brick_layout(key):
    base_key = jax.random.fold_in(key, 101)
    key_full, key_perm, key_x, key_y, key_z = jax.random.split(base_key, 5)
    rows_x = NB // NBX
    owners = NB // NBY
    favored = jax.random.randint(key_full, (rows_x,), 0, owners)
    part_index = jnp.arange(PARTITIONS, dtype=jnp.int32)
    part_row = part_index // owners
    spare_slots = BLK_DEV - CAP
    perm_keys = jax.random.split(key_perm, PARTITIONS)
    shuffled = jax.vmap(lambda one_key: jax.random.permutation(one_key, spare_slots))(perm_keys)
    shuffled = shuffled.astype(jnp.int32) + CAP
    leading = jnp.broadcast_to(jnp.arange(CAP, dtype=jnp.int32)[None, :], (PARTITIONS, CAP))
    slot_order = jnp.concatenate([leading, shuffled], axis=1)
    target = (slot_order // CAP + favored[part_row][:, None]) % owners
    local_x = jax.random.randint(key_x, (PARTITIONS, BLK_DEV), 0, NBX)
    local_y = jax.random.randint(key_y, (PARTITIONS, BLK_DEV), 0, NBY)
    local_z = jax.random.randint(key_z, (PARTITIONS, BLK_DEV), 0, NB)
    brick_x = part_row[:, None] * NBX + local_x
    brick_y = target * NBY + local_y
    return ((brick_x * NB + brick_y) * NB + local_z).reshape(NBLK).astype(jnp.int32)


def draw_block_brick(key, part):
    return brick_layout(key)


def draw_positions(key, part):
    bricks = brick_layout(key)
    corners = jnp.stack([bricks // (NB * NB), bricks // NB % NB, bricks % NB]).astype(jnp.float32) * B
    spread = jax.random.uniform(jax.random.fold_in(key, 202), (3, NBLK, PB), dtype=jnp.float32)
    placed = corners[:, :, None] + 0.5 + (B - 1.0) * spread
    return placed.reshape(3, NPTS)


def draw_block_count(key, part):
    base_key = jax.random.fold_in(key, 303)
    key_a, key_b, key_c, key_d = jax.random.split(base_key, 4)
    spare_slots = BLK_DEV - CAP
    factor_one = jax.random.randint(key_a, (PARTITIONS,), 0, spare_slots + 1)
    factor_two = jax.random.randint(key_b, (PARTITIONS,), 0, spare_slots + 1)
    counts = BLK_DEV // 2 + factor_one * factor_two // (2 * spare_slots)
    fullest = jax.random.randint(key_c, (), 0, PARTITIONS)
    emptiest = (fullest + 1 + jax.random.randint(key_d, (), 0, PARTITIONS - 1)) % PARTITIONS
    counts = counts.at[fullest].set(BLK_DEV).at[emptiest].set(CAP)
    return counts.astype(jnp.int32)


def block_levels(key, shape, cuts, smallest, high):
    def one(dim, parts):
        heights = jax.random.uniform(jax.random.fold_in(jax.random.fold_in(key, 6), dim), (parts,), jnp.float32, smallest / len(cuts), high / len(cuts))
        return jnp.repeat(jnp.exp(heights), shape[dim] // parts).reshape((-1,) + (1,) * (len(shape) - dim - 1))

    factor_of = one(*cuts[0])
    for cut in cuts[1:]:
        factor_of = factor_of * one(*cut)
    return factor_of


def centred(stream_key, extent, width, limit, cuts=(), kind=jnp.bfloat16):
    factor_of = block_levels(stream_key, extent, cuts, -0.22, 0.18) if cuts else 1.0
    entries = jax.random.normal(stream_key, extent, jnp.float32) * width * factor_of
    return jnp.minimum(jnp.maximum(entries, -limit), limit).astype(kind)


def setup_inputs(seed: int = 0) -> dict:
    splits = jax.random.split(jax.random.key(seed), 12)
    return {
        "positions": draw_positions(jax.random.fold_in(splits[11], 71), 0),
        "point_feat": centred(splits[1], (C, NPTS), 0.3, 1.8, ((1, 128),), jnp.float32),
        "area": jnp.clip(jnp.exp(math.log(3.0) - 2.3025851 * jax.random.uniform(splits[2], (NPTS,), jnp.float32) ** block_levels(splits[2], (NPTS,), ((0, 128),), -0.2, 0.2)), 0.3, 3.0),
        "block_brick": draw_block_brick(jax.random.fold_in(splits[11], 71), 0),
        "block_count": draw_block_count(jax.random.fold_in(splits[11], 71), 0),
        "sdf": centred(splits[5], (G, G, G), 1.0, 6.0, ((0, 8), (1, 16)), jnp.float32),
        "grid_gain": centred(splits[6], (C,), 1.0, 4.0, (), jnp.float32),
        "mix_w": centred(splits[7], (LAYERS, C, C), C ** -0.5, 1.0, (), jnp.float32),
        "mix_b": centred(splits[8], (LAYERS, C), 0.3, 1.8, (), jnp.float32),
        "spec_w": centred(splits[9], (LAYERS, 2, KZ, C, M * M), 3.0, 18.0, ((2, 16), (3, 8)), jnp.float32),
        "readout_w": centred(splits[10], (C,), C ** -0.5, 1.0, (), jnp.float32),
    }


highest = lax.Precision.HIGHEST


def cell_offsets(brick_edge):
    cell_index = jnp.arange(brick_edge * brick_edge * brick_edge, dtype=jnp.int32)
    coords = jnp.stack([cell_index // (brick_edge * brick_edge), (cell_index // brick_edge) % brick_edge, cell_index % brick_edge])
    return coords.astype(jnp.float32) + 0.5


def kernel_weights(corners, points, offsets, radius):
    distance = jnp.zeros((corners.shape[0], offsets.shape[1], points.shape[2]), dtype=points.dtype)
    for axis_id in range(3):
        centre_line = corners[:, axis_id][:, None] + offsets[axis_id][None, :]
        gap_line = centre_line[:, :, None] - points[:, axis_id][:, None, :]
        distance = distance + gap_line * gap_line
    return jnp.square(jnp.maximum(1.0 - distance / (radius * radius), 0.0))


def spectral_channel(values, weights):
    half_modes = M // 2
    spectrum = jnp.fft.rfftn(values)
    spectrum = jnp.concatenate([spectrum[:half_modes], spectrum[G - half_modes:]], axis=0)
    spectrum = jnp.concatenate([spectrum[:, :half_modes], spectrum[:, G - half_modes:]], axis=1)
    spectrum = spectrum[:, :, :KZ]
    factor = (weights[0] + 1j * weights[1]).reshape(KZ, M, M).transpose(1, 2, 0)
    scaled = spectrum * factor
    padded = jnp.zeros((G, G, G // 2 + 1), dtype=scaled.dtype)
    padded = padded.at[:half_modes, :half_modes, :KZ].set(scaled[:half_modes, :half_modes])
    padded = padded.at[:half_modes, G - half_modes:, :KZ].set(scaled[:half_modes, half_modes:])
    padded = padded.at[G - half_modes:, :half_modes, :KZ].set(scaled[half_modes:, :half_modes])
    padded = padded.at[G - half_modes:, G - half_modes:, :KZ].set(scaled[half_modes:, half_modes:])
    return jnp.fft.irfftn(padded, s=(G, G, G))


def reference(positions, point_feat, area, block_brick, block_count, sdf, grid_gain, mix_w, mix_b, spec_w, readout_w):
    side_bricks = G // B
    cell_count = B * B * B
    block_index = jnp.arange(NBLK, dtype=jnp.int32)
    live_mask = (block_index % BLK_DEV) < block_count[block_index // BLK_DEV]
    live_scale = jnp.where(live_mask, 1.0, 0.0).astype(positions.dtype)
    brick_x = block_brick // (side_bricks * side_bricks)
    brick_y = (block_brick // side_bricks) % side_bricks
    brick_z = block_brick % side_bricks
    corners = jnp.stack([brick_x, brick_y, brick_z], axis=1).astype(positions.dtype) * B
    block_pos = positions.reshape(3, NBLK, PB).transpose(1, 0, 2)
    block_feat = point_feat.reshape(C, NBLK, PB).transpose(1, 0, 2) * area.reshape(NBLK, 1, PB)
    offsets = cell_offsets(B).astype(positions.dtype)
    group_count = NBLK // BLK_DEV
    grouped = (corners.reshape(group_count, BLK_DEV, 3), block_pos.reshape(group_count, BLK_DEV, 3, PB),
               block_feat.reshape(group_count, BLK_DEV, C, PB), block_brick.reshape(group_count, BLK_DEV),
               live_scale.reshape(group_count, BLK_DEV))

    def encode_step(bricks, group_items):
        corner_set, point_set, feature_set, brick_ids, scale_set = group_items
        weights = kernel_weights(corner_set, point_set, offsets, B)
        contrib = jnp.einsum("rcp,rgp->rcg", feature_set, weights, precision=highest) * scale_set[:, None, None]
        return bricks.at[brick_ids].add(contrib.reshape(BLK_DEV, C * cell_count)), None

    bricks = jnp.zeros((side_bricks ** 3, C * cell_count), dtype=positions.dtype)
    bricks, unused = lax.scan(encode_step, bricks, grouped)
    grid_field = bricks.reshape(side_bricks, side_bricks, side_bricks, C, B, B, B).transpose(3, 0, 4, 1, 5, 2, 6).reshape(C, G, G, G)
    grid_field = grid_field + grid_gain[:, None, None, None] * sdf[None]

    def channel_step(channel_items):
        return spectral_channel(channel_items[0], channel_items[1])

    for layer_index in range(LAYERS):
        per_channel = spec_w[layer_index].transpose(2, 0, 1, 3)
        spectral = lax.map(channel_step, (grid_field, per_channel))
        mixed_sum = jnp.einsum("oc,cxyz->oxyz", mix_w[layer_index], grid_field, precision=highest)
        mixed_sum = mixed_sum + mix_b[layer_index][:, None, None, None] + spectral
        grid_field = jax.nn.gelu(mixed_sum) if layer_index < LAYERS - 1 else mixed_sum

    final_bricks = grid_field.reshape(C, side_bricks, B, side_bricks, B, side_bricks, B).transpose(1, 3, 5, 0, 2, 4, 6)
    final_bricks = final_bricks.reshape(side_bricks ** 3, C * cell_count)

    def decode_group(group_items):
        corner_set, point_set, brick_ids = group_items
        weights = kernel_weights(corner_set, point_set, offsets, B)
        brick_vals = final_bricks[brick_ids].reshape(BLK_DEV, C, cell_count)
        decoded = jnp.einsum("rcg,rgp->rcp", brick_vals, weights, precision=highest) / jnp.sum(weights, axis=1)[:, None, :]
        return jnp.einsum("c,rcp->rp", readout_w, decoded, precision=highest)

    pressure = lax.map(decode_group, (grouped[0], grouped[1], grouped[3])).reshape(NBLK, PB)
    return jnp.where(live_mask[:, None], pressure, 0.0).reshape(NPTS)
```

```python
import functools

import jax
import jax.numpy as jnp
import ml_dtypes
import numpy as np
from jax import lax
from jax.experimental import pallas as pl
from jax.experimental.pallas import tpu as pltpu
from jax.sharding import PartitionSpec as P

MESH = pl.DeviceIdType.MESH
F32 = jnp.float32
BF16 = jnp.bfloat16

G = 128
M = 32
KZ = 16
NX = 8
NY = 16
CAP = 8
SLOTS = NY * CAP
ROWS = CAP * 32 + 3 * CAP
POINTS = [(t % 4, (t % 4 + t // 4) % 4) for t in range(16)]
FAR = [(2, 2), (2, 1), (1, 2), (2, 3), (3, 2), (1, 1), (3, 3), (3, 1), (1, 3), (2, 0), (0, 2), (0, 1), (1, 0), (0, 3), (3, 0), (0, 0)]


def split_table(table):
    high = table.astype(ml_dtypes.bfloat16)
    low = (table - high.astype(np.float64)).astype(ml_dtypes.bfloat16)
    return high, low


def tables():
    place = np.arange(G)
    kz = np.arange(KZ)
    m = np.arange(M)
    freq = np.where(m < M // 2, m, m - M)
    za = 2.0 * np.pi * (np.outer(kz, place) % G) / G
    fa = 2.0 * np.pi * (np.outer(place, freq) % G) / G
    c, s = np.cos(fa), np.sin(fa)
    zf_h, zf_l = split_table(np.concatenate([np.cos(za), -np.sin(za)], 0))
    zero = np.zeros_like(zf_h)
    zf = np.block([[zf_h, zf_h], [zf_l, zero]])
    yf_h, yf_l = split_table(np.block([[c, -s], [s, c]]))
    yf = np.block([[yf_h, yf_l], [yf_h, np.zeros_like(yf_l)]])
    xf_h, xf_l = split_table(np.concatenate([c.T, s.T], 1))
    xf = np.concatenate([xf_h, xf_l], 0)
    xi_h, xi_l = split_table(np.concatenate([c, s], 1) / G)
    xi = np.concatenate([xi_h, xi_l], 1)
    yi_h, yi_l = split_table(np.block([[c.T, s.T], [-s.T, c.T]]) / G)
    yi = np.concatenate([yi_h, yi_h, yi_l, yi_l], 0)
    back = np.where(kz == 0, 1.0, 2.0)[:, None] / G
    zi_h, zi_l = split_table(np.concatenate([np.cos(za) * back, -np.sin(za) * back], 0).T)
    zi = np.concatenate([zi_h, zi_h, zi_l, zi_l], 1)

    def spread(t):
        return np.repeat(t.reshape(G, 2, KZ).transpose(0, 2, 1), NX, axis=1).reshape(G, 2 * KZ * NX)

    zs = np.concatenate([spread(zi_h), spread(zi_h), spread(zi_l)], 1)
    return [jnp.asarray(t, BF16) for t in (zf, yf, xf, xi, yi, zi, zs)]


def dot(a, b):
    return jnp.dot(a, b, preferred_element_type=F32)


def split(value):
    high = value.astype(BF16)
    low = (value - high.astype(F32)).astype(BF16)
    return high, low


def split3(value):
    high = value.astype(BF16)
    rest = value - high.astype(F32)
    mid = rest.astype(BF16)
    return high, mid, (rest - mid.astype(F32)).astype(BF16)


def pick(chosen, value):
    return dot(chosen, jnp.concatenate(split3(value), axis=0))


def lanes(shape):
    return lax.broadcasted_iota(jnp.int32, shape, len(shape) - 1)


def split_lanes(value):
    high = value.astype(BF16).astype(F32)
    return jnp.where(lanes(value.shape) < 64, high, value - high).astype(BF16)


def fold(value):
    return value + pltpu.roll(value, 64, 1)


def swap16(tiles):
    group = lanes(tiles[0].shape) // 8
    for d in (1, 2, 4, 8):
        mask = (group // d) % 2 == 0
        new = list(tiles)
        for i in range(16):
            if i & d:
                continue
            a, b = tiles[i], tiles[i + d]
            new[i] = jnp.where(mask, a, pltpu.roll(b, 8 * d, 1))
            new[i + d] = jnp.where(mask, pltpu.roll(a, G - 8 * d, 1), b)
        tiles = new
    return tiles


def kernel_tiles(px, py, pz):
    def local(p):
        q = p * 0.125
        return jnp.broadcast_to(q - jnp.floor(q), (8, 128))

    ux, uy, uz = local(px), local(py), local(pz)
    centre = (lax.broadcasted_iota(jnp.int32, (8, 128), 0).astype(F32) + 0.5) * 0.125
    gap = centre - uy
    base = 1.0 - gap * gap
    ex, ez = [], []
    for a in range(8):
        gx = (a + 0.5) * 0.125 - ux
        ex.append(gx * gx)
        gz = (a + 0.5) * 0.125 - uz
        ez.append(base - gz * gz)
    out = []
    for z in range(8):
        for x in range(8):
            t = jnp.maximum(ez[z] - ex[x], 0.0)
            out.append(t * t)
    return out


def points_offset(t):
    step = lax.rem(t, 4)
    return step, lax.rem(step + t // 4, 4)


def mega(
    brick, count, feat, pos, area, sdf, gain, mix, bias, spec, readout, zf_h, yf_h, xf_h, xi_h, yi_h, zi_h, zs_h,
    out,
    zf, yf, xf, xi, yi, zi, zs,
    brickv, counts, posv, areav, sdfv, gains, mixv, biases, specv, readouts,
    vecv, vecs, mixf, mixt, wbuf, homes, placed,
    sbuf, rbuf, msend, mrecv, kst, contr, g, mixed, sdft,
    send, frecv, irecv, frecv1, jsend, jrecv, plane, sacc, srow, psend, precv,
    insem, featsem, bsem, psem, msem, osem, fsem, isem, f1sem, jsem, rsem, entered,
):
    gx = lax.axis_index("gx")
    gy = lax.axis_index("gy")
    me = gx * NY + gy
    cy, core = gx // 2, lax.rem(gx, 2)
    cz, cx = gy // 4, lax.rem(gy, 4)

    def peer(dz, dx):
        return lax.rem(cz + dz, 4) * 4 + lax.rem(cx + dx, 4)

    small = [
        (brick, brickv), (count, counts), (pos, posv), (area, areav), (readout, readouts), (mix, mixv), (bias, biases),
        (gain, gains), (spec, specv), (sdf, sdfv),
        (zf_h, zf), (yf_h, yf), (xf_h, xf), (xi_h, xi), (yi_h, yi), (zi_h, zi), (zs_h, zs),
    ]
    loads = [pltpu.make_async_copy(a, b, insem.at[i]) for i, (a, b) in enumerate(small)]
    for load in loads[:4]:
        load.start()

    barrier = pltpu.get_barrier_semaphore()
    for t in range(1, NY):
        pl.semaphore_signal(barrier, inc=1, device_id=(gx, lax.rem(gy + t, NY)), device_id_type=MESH)
    for t in range(1, NX):
        pl.semaphore_signal(barrier, inc=1, device_id=(lax.rem(gx + t, NX), gy), device_id_type=MESH)

    def load_feat(n, carry):
        pltpu.make_async_copy(
            feat.at[:, pl.ds(pl.multiple_of(n * 128, 128), 128)],
            mixed.at[pl.ds(pl.multiple_of(n * 32, 32), 32), :], featsem,
        ).start()
        return carry

    lax.fori_loop(0, SLOTS, load_feat, 0)
    for load in loads[4:]:
        load.start()

    sub = lax.broadcasted_iota(jnp.int32, (G, G), 0)
    lane = lanes((G, G))
    one = jnp.ones((G, G), jnp.int32)
    zero = jnp.zeros((G, G), jnp.int32)

    def total(value):
        return jnp.sum(value, axis=0, keepdims=True)

    loads[0].wait()
    loads[1].wait()
    blocks = jnp.broadcast_to(brickv[...], (G, G))
    live_blocks = counts[0]
    owner = lax.shift_right_logical(blocks, 4) & 15
    inner = (lax.shift_right_logical(blocks, 8) & 1) * 16 + (blocks & 15)
    owner_t = jnp.transpose(owner)
    ahead = (owner_t == owner) & (sub < lane) & (sub < live_blocks)
    slot = jnp.where(lane[0:1] < live_blocks, owner[0:1] * CAP + total(jnp.where(ahead, one, zero)), SLOTS)
    match = jnp.where(jnp.transpose(jnp.broadcast_to(slot, (G, G))) == lane, one, zero)
    bricks = jnp.where(total(match) > 0, total(match * jnp.transpose(inner)), 32)
    msend[...] = jnp.transpose(jnp.broadcast_to(bricks, (G, G)))
    mine = pl.ds(pl.multiple_of(gy * CAP, CAP), CAP)
    mrecv[mine, :] = msend[mine, :]
    back_home = match.astype(F32).astype(BF16)
    homes[...] = jnp.concatenate([back_home] * 3, axis=1)
    to_slot = jnp.transpose(match).astype(F32).astype(BF16)
    placed[...] = jnp.concatenate([to_slot] * 3, axis=1)

    loads[2].wait()
    loads[3].wait()
    pltpu.make_async_copy(mixed, mixed, featsem).wait()

    areas = jnp.concatenate([areav[:, 128 * n : 128 * n + 128] for n in range(SLOTS)], axis=0)
    scale = pick(placed[...], areas)

    def pack(c, carry):
        h, l = split(mixed[pl.ds(c, SLOTS, stride=32), :])
        o = dot(placed[:, 0:256], jnp.concatenate([h, l], axis=0)) * scale
        for j in range(NY):
            sbuf[j, pl.ds(c, CAP, stride=32), :] = o[CAP * j : CAP * j + CAP]
        return carry

    lax.fori_loop(0, 32, pack, 0, unroll=2)
    for k in range(3):
        o = pick(placed[...], jnp.concatenate([posv[k : k + 1, 128 * n : 128 * n + 128] for n in range(SLOTS)], axis=0))
        for j in range(NY):
            sbuf[j, 256 + 8 * k : 264 + 8 * k, :] = o[CAP * j : CAP * j + CAP]
    pl.semaphore_wait(barrier, NY + NX - 2)

    for dz, dx in POINTS[1:]:
        j = peer(dz, dx)
        pltpu.make_async_remote_copy(
            src_ref=msend.at[pl.ds(pl.multiple_of(j * CAP, CAP), CAP), :], dst_ref=mrecv.at[mine, :],
            send_sem=msem.at[0], recv_sem=msem.at[1], device_id=(gx, j), device_id_type=MESH,
        ).start()
    for dz, dx in POINTS[1:]:
        j = peer(dz, dx)
        pltpu.make_async_remote_copy(
            src_ref=sbuf.at[j], dst_ref=rbuf.at[gy],
            send_sem=bsem, recv_sem=psem.at[gy], device_id=(gx, j), device_id_type=MESH,
        ).start()
    for t in range(1, NX):
        pl.semaphore_signal(entered, inc=1, device_id=(lax.rem(gx + t, NX), gy), device_id_type=MESH)
    rbuf[gy] = sbuf[gy]

    for load in loads[4:]:
        load.wait()
    sdft[...] = jnp.transpose(sdfv[...])
    vec = jnp.zeros((1, 32), F32)
    shift = jnp.float32(0.0)
    for o in range(32):
        vec = vec + readouts[o] * mixv[1, o : o + 1, :]
        shift = shift + readouts[o] * biases[1, o]
    vecv[:, 0:32] = vec
    vec_copy = pltpu.make_async_copy(vecv, vecs, osem)
    vec_copy.start()
    for k in range(4):
        mixf[:, 32 * k : 32 * k + 32] = mixv[0]
    mixt[...] = split_lanes(mixf[...])
    narrow = lanes((8, 128)) < 32
    for layer in range(2):
        pair = jnp.concatenate([specv[2 * layer], specv[2 * layer + 1]], axis=0)
        for t in range(8):
            part = pair[:, 128 * t : 128 * t + 128]
            for u in range(4):
                w = jnp.where(narrow, part if u == 0 else pltpu.roll(part, G - 32 * u, 1), 0.0)
                w = w + pltpu.roll(w, 32, 1)
                wbuf[layer * 256 + (4 * t + u) * 8 : layer * 256 + (4 * t + u) * 8 + 8, :] = w + pltpu.roll(w, 64, 1)
    vec_copy.wait()

    whole = mrecv.at[pl.ds(0, (NY - 1) * CAP), :]
    pltpu.make_async_copy(whole, whole, msem.at[0]).wait()
    pltpu.make_async_copy(whole, whole, msem.at[1]).wait()
    inside = jnp.where(jnp.transpose(mrecv[...])[0:32] == sub[0:32], 1.0, 0.0).astype(BF16)
    inside = jnp.concatenate([inside, inside], axis=1)

    def encode(t, carry):
        dz, dx = points_offset(t)
        j = lax.rem(cz + 4 - dz, 4) * 4 + lax.rem(cx + 4 - dx, 4)

        @pl.when(t > 0)
        def _():
            pltpu.make_async_copy(rbuf.at[j], rbuf.at[j], psem.at[j]).wait()

        for i in range(CAP):
            tiles = kernel_tiles(
                rbuf[j, 256 + i : 257 + i, :], rbuf[j, 264 + i : 265 + i, :], rbuf[j, 272 + i : 273 + i, :]
            )
            kh, kl = split(jnp.concatenate(tiles, axis=0))
            fh, fl = split(rbuf[j, 32 * i : 32 * i + 32, :])
            lhs = jnp.concatenate(
                [jnp.concatenate([fh, fh], axis=1), jnp.concatenate([fl, jnp.zeros_like(fl)], axis=1)], axis=0
            )
            rhs = jnp.concatenate([kh, kl], axis=1)
            kst[j * CAP + i] = rhs
            o = lax.dot_general(lhs, rhs, (((1,), (1,)), ((), ())), preferred_element_type=F32)
            o = o[0:32] + o[32:64]
            for q in range(4):
                contr[q, pl.ds(pl.multiple_of((j * CAP + i) * 32, 32), 32), :] = o[:, 128 * q : 128 * q + 128]
        return carry

    lax.fori_loop(0, NY, encode, 0)

    low = lanes((16, 128)) < 64

    def assemble(c, carry):
        for q in range(4):
            h, l = split(contr[q, pl.ds(c, SLOTS, stride=32), :])
            o = dot(inside, jnp.concatenate([h, l], axis=0))
            a, b = o[0:16], o[16:32]
            g[pl.ds(c * G + 2 * q, 16, stride=8), :] = jnp.where(low, a, pltpu.roll(b, 64, 1))
            g[pl.ds(c * G + 2 * q + 1, 16, stride=8), :] = jnp.where(low, pltpu.roll(a, 64, 1), b)
        return carry

    lax.fori_loop(0, 32, assemble, 0, unroll=2)
    pl.semaphore_wait(entered, NX - 1)

    def group_of(t):
        u = t // 2
        dy = lax.rem(2 + 3 * u + 3 * (u // 2) + 2 * (u // 3), 4)
        return lax.rem(cy + dy, 4) * 2 + lax.rem(core + 1 + lax.rem(t, 2), 2)

    partners = [peer(dz, dx) for dz, dx in FAR]

    def issue(t, grp, source_row, recv, row, size, sem):
        for n, k in enumerate(partners):
            copy = pltpu.make_async_remote_copy(
                src_ref=send.at[pl.ds(pl.multiple_of(source_row(k), size), size), :] if size == 8
                else jsend.at[pl.ds(pl.multiple_of(source_row(k), size), size), :],
                dst_ref=recv.at[pl.ds(pl.multiple_of(row, size), size), :],
                send_sem=sem.at[0], recv_sem=sem.at[1], device_id=(grp, k), device_id_type=MESH,
            )
            if n < NY - 1:
                copy.start()
            else:
                pl.when(t < NX - 1)(copy.start)

    def forward(recv, sem, prepare):
        def group(t, carry):
            grp = group_of(t)
            for ci in range(4):
                c = grp * 4 + ci
                rows = pl.ds(pl.multiple_of(c * G, G), G)
                value = prepare(c, rows)
                h, l = split(value)
                o = dot(zf[...], jnp.concatenate([h, l], axis=0))
                o = o[0:32] + o[32:64]
                for ri in range(2):
                    send[pl.ds(grp * 8 + ri * 4 + ci, 16, stride=64), :] = o[16 * ri : 16 * ri + 16]
            issue(t, grp, lambda k: (k * NX + grp) * 8, recv, me * 8, 8, sem)
            return carry

        lax.fori_loop(0, NX, group, 0)
        recv[pl.ds(pl.multiple_of(me * 8, 8), 8), :] = send[pl.ds(pl.multiple_of((gy * NX + gx) * 8, 8), 8), :]

    def arrive(recv, sem, size=8):
        part = recv.at[pl.ds(0, (NX * NY - 1) * size), :]
        pltpu.make_async_copy(part, part, sem.at[1]).wait()
        pltpu.make_async_copy(part, part, sem.at[0]).wait()

    sign_f = jnp.where(lanes((1, 128)) % 64 < 32, 1.0, -1.0)

    def modes(recv, layer):
        for a in range(NX):
            tiles = [recv[(a * 16 + b) * 8 : (a * 16 + b) * 8 + 8, :] for b in range(16)]
            tiles = swap16(tiles)
            for b in range(16):
                plane[(a * 16 + b) * 8 : (a * 16 + b) * 8 + 8, :] = tiles[b]
        result = []
        for ci in range(4):
            both = jnp.concatenate(
                [plane[pl.ds(ci, G, stride=8), :], plane[pl.ds(4 + ci, G, stride=8), :]], axis=1
            )
            h, l = split(both)
            y = fold(dot(jnp.concatenate([h, l], axis=1), yf[...]))
            y2 = pltpu.roll(y, 96, 1) * sign_f
            z = dot(xf[...], jnp.concatenate([split_lanes(y), split_lanes(y2)], axis=0))
            z = fold(z[0:32] + z[32:64])
            wr = wbuf[pl.ds(layer * 256 + ci, M, stride=8), :]
            wi = wbuf[pl.ds(layer * 256 + 4 + ci, M, stride=8), :]
            result.append(z * wr - pltpu.roll(z, 96, 1) * (wi * sign_f))
        return result

    def inverse_plane(p):
        p2 = pltpu.roll(p, 96, 1) * (-sign_f)
        r = jnp.concatenate([split_lanes(p), split_lanes(p2)], axis=0)
        q = split_lanes(fold(dot(xi[...], jnp.concatenate([r, r], axis=0))))
        return dot(jnp.concatenate([q, q], axis=1), yi[...])

    def prepare0(c, rows):
        value = g[rows, :] + gains[c] * sdft[...]
        g[rows, :] = value
        return value

    forward(frecv, fsem, prepare0)

    def mix_cells(z, carry):
        h, l = split(g[pl.ds(z, 32, stride=G), :])
        mixed[pl.ds(z, 32, stride=G), :] = dot(mixt[...], jnp.concatenate([h, l, h, l], axis=0))
        return carry

    lax.fori_loop(0, G, mix_cells, 0, unroll=4)
    arrive(frecv, fsem)
    for ci, p in enumerate(modes(frecv, 0)):
        o = inverse_plane(p)
        plane[pl.ds(ci, G, stride=8), :] = o[:, 0:128]
        plane[pl.ds(ci + 4, G, stride=8), :] = o[:, 128:256]

    spot = gy * NX + gx

    def back(t, carry):
        grp = group_of(t)
        base = pl.multiple_of(grp * 128, 128)
        tiles = swap16([plane[pl.ds(base + 8 * b, 8), :] for b in range(16)])
        for b in range(16):
            send[pl.ds(base + 8 * b, 8), :] = tiles[b]
        issue(t, grp, lambda k: (grp * NY + k) * 8, irecv, spot * 8, 8, isem)
        return carry

    lax.fori_loop(0, NX, back, 0)
    irecv[pl.ds(pl.multiple_of(spot * 8, 8), 8), :] = send[pl.ds(pl.multiple_of(me * 8, 8), 8), :]
    arrive(irecv, isem)
    sacc[...] = jnp.zeros_like(sacc) + shift

    def prepare1(c, rows):
        grp, ci = c // 4, lax.rem(c, 4)
        re = irecv[pl.ds(grp * 8 + ci, 16, stride=64), :]
        im = irecv[pl.ds(grp * 8 + 4 + ci, 16, stride=64), :]
        h, l = split(jnp.concatenate([re, im], axis=0))
        value = dot(zi[...], jnp.concatenate([h, l, h, l], axis=0)) + mixed[rows, :] + biases[0, c]
        value = jax.nn.gelu(value)
        sacc[...] += vecs[0, c] * value
        return value

    forward(frecv1, f1sem, prepare1)
    arrive(frecv1, f1sem)
    projected = None
    for ci, p in enumerate(modes(frecv1, 1)):
        p = p * readouts[gx * 4 + ci]
        projected = p if projected is None else projected + p
    o = inverse_plane(projected)
    for a in range(NX):
        for ri in range(2):
            plane[pl.ds((a // 4) * 128 + (a % 4) * 2 + ri, 16, stride=8), :] = o[16 * a : 16 * a + 16, 128 * ri : 128 * ri + 128]
    for half in range(2):
        tiles = swap16([plane[half * 128 + 8 * b : half * 128 + 8 * b + 8, :] for b in range(16)])
        for b in range(16):
            jsend[half * 128 + 8 * b : half * 128 + 8 * b + 8, :] = tiles[b]

    def back1(t, carry):
        grp = group_of(t)
        issue(t, grp, lambda k: ((grp // 4) * 16 + k) * 8 + lax.rem(grp, 4) * 2, jrecv, spot * 2, 2, jsem)
        return carry

    lax.fori_loop(0, NX, back1, 0)
    jrecv[pl.ds(pl.multiple_of(spot * 2, 2), 2), :] = jsend[
        pl.ds(pl.multiple_of(((gx // 4) * 16 + gy) * 8 + lax.rem(gx, 4) * 2, 2), 2), :
    ]
    arrive(jrecv, jsem, 2)
    h, l = split(jrecv[...])
    field = sacc[...] + dot(zs[...], jnp.concatenate([h, l, h], axis=0))

    left = lanes((16, 128)) < 64
    sacc[...] = field
    for q in range(4):
        a = sacc[pl.ds(2 * q, 16, stride=8), :]
        b = sacc[pl.ds(2 * q + 1, 16, stride=8), :]
        for bx in range(2):
            w = jnp.where(left, a, pltpu.roll(b, 64, 1)) if bx == 0 else jnp.where(left, pltpu.roll(a, 64, 1), b)
            h, l = split(w)
            srow[16 * bx : 16 * bx + 16, 128 * q : 128 * q + 128] = h
            srow[32 + 16 * bx : 48 + 16 * bx, 128 * q : 128 * q + 128] = l
    srow[64:80, :] = jnp.ones((16, 512), BF16)
    which = sub[0:32]

    def decode(j, carry):
        nums, dens = [], []
        for i in range(CAP):
            o = dot(srow[...], kst[j * CAP + i])
            o = o[0:72, 0:128] + o[0:72, 128:256]
            owned = jnp.broadcast_to(mrecv[pl.ds(j * CAP + i, 1), :], (32, 128)) == which
            nums.append(total(jnp.where(owned, o[0:32] + o[32:64], 0.0)))
            dens.append(o[64:65])
        psend[pl.ds(pl.multiple_of(j * CAP, CAP), CAP), :] = jnp.concatenate(nums, axis=0) / jnp.concatenate(dens, axis=0)
        return carry

    lax.fori_loop(0, NY, decode, 0)
    precv[mine, :] = psend[mine, :]
    for dz, dx in FAR[:-1]:
        j = peer(dz, dx)
        pltpu.make_async_remote_copy(
            src_ref=psend.at[pl.ds(pl.multiple_of(j * CAP, CAP), CAP), :], dst_ref=precv.at[mine, :],
            send_sem=rsem.at[0], recv_sem=rsem.at[1], device_id=(gx, j), device_id_type=MESH,
        ).start()
    part = precv.at[pl.ds(0, (NY - 1) * CAP), :]
    pltpu.make_async_copy(part, part, rsem.at[1]).wait()
    pltpu.make_async_copy(part, part, rsem.at[0]).wait()
    sent = sbuf.at[pl.ds(0, NY - 1)]
    pltpu.make_async_copy(sent, sent, bsem).wait()

    out[...] = pick(homes[...], precv[...])


def per_device(positions, point_feat, area, block_brick, block_count, sdf, grid_gain, mix_w, mix_b, spec_w, readout_w):
    consts = tables()
    hbm = pl.BlockSpec(memory_space=pl.ANY)
    dma = pltpu.SemaphoreType.DMA
    vmem = pltpu.VMEM
    i32 = jnp.int32
    out = pl.pallas_call(
        mega,
        out_shape=jax.ShapeDtypeStruct((SLOTS, 128), F32),
        in_specs=[hbm] * (11 + len(consts)),
        out_specs=pl.BlockSpec(memory_space=vmem),
        scratch_shapes=[vmem(t.shape, BF16) for t in consts]
        + [
            vmem((1, SLOTS), i32),
            pltpu.SMEM((1,), i32),
            vmem((3, SLOTS * 128), F32),
            vmem((1, SLOTS * 128), F32),
            vmem((G, 128), F32),
            pltpu.SMEM((32,), F32),
            vmem((2, 32, 32), F32),
            pltpu.SMEM((2, 32), F32),
            vmem((4, 4, M * M), F32),
            pltpu.SMEM((32,), F32),
            vmem((1, 128), F32),
            pltpu.SMEM((1, 128), F32),
            vmem((32, 128), F32),
            vmem((32, 128), BF16),
            vmem((512, 128), F32),
            vmem((SLOTS, 384), BF16),
            vmem((SLOTS, 384), BF16),
            vmem((NY, ROWS, 128), F32),
            vmem((NY, ROWS, 128), F32),
            vmem((SLOTS, 128), i32),
            vmem((SLOTS, 128), i32),
            vmem((SLOTS, 512, 256), BF16),
            vmem((4, SLOTS * 32, 128), F32),
            vmem((32 * G, 128), F32),
            vmem((32 * G, 128), F32),
            vmem((G, 128), F32),
            vmem((1024, 128), F32),
            vmem((1024, 128), F32),
            vmem((1024, 128), F32),
            vmem((1024, 128), F32),
            vmem((256, 128), F32),
            vmem((256, 128), F32),
            vmem((1024, 128), F32),
            vmem((G, 128), F32),
            vmem((80, 512), BF16),
            vmem((SLOTS, 128), F32),
            vmem((SLOTS, 128), F32),
            dma((10 + len(consts),)), dma, dma, dma((NY,)), dma((2,)), dma, dma((2,)), dma((2,)), dma((2,)),
            dma((2,)), dma((2,)), pltpu.SemaphoreType.REGULAR,
        ],
        compiler_params=pltpu.CompilerParams(collective_id=0, has_side_effects=True, vmem_limit_bytes=67043328),
        name="operator",
    )(
        block_brick.reshape(1, SLOTS), block_count, point_feat, positions, area.reshape(1, SLOTS * 128), sdf.reshape(G, 128),
        grid_gain, mix_w, mix_b, spec_w.reshape(4, 4, M * M), readout_w, *consts,
    )
    return out.reshape(SLOTS * 128)


def solution(mesh):
    placed = (
        P(None, ("gx", "gy")),
        P(None, ("gx", "gy")),
        P(("gx", "gy")),
        P(("gx", "gy")),
        P(("gx", "gy")),
        P("gx", "gy", None),
        P(),
        P(),
        P(),
        P(None, None, "gy", "gx", None),
        P(),
    )
    return jax.shard_map(per_device, mesh=mesh, in_specs=placed, out_specs=P(("gx", "gy")), check_vma=False)
```

```python
import functools

import jax
import jax.numpy as jnp
import ml_dtypes
import numpy as np
from jax import lax
from jax.experimental import pallas as pl
from jax.experimental.pallas import tpu as pltpu
from jax.sharding import PartitionSpec as P

MESH = pl.DeviceIdType.MESH
F32 = jnp.float32
BF16 = jnp.bfloat16

G = 128
M = 32
KZ = 16
NX = 8
NY = 16
CAP = 8
SLOTS = NY * CAP
ROWS = CAP * 32 + 3 * CAP
POINTS = [(t % 4, (t % 4 + t // 4) % 4) for t in range(16)]
FAR = [(2, 2), (2, 1), (1, 2), (2, 3), (3, 2), (1, 1), (3, 3), (3, 1), (1, 3), (2, 0), (0, 2), (0, 1), (1, 0), (0, 3), (3, 0), (0, 0)]


def split_table(table):
    high = table.astype(ml_dtypes.bfloat16)
    low = (table - high.astype(np.float64)).astype(ml_dtypes.bfloat16)
    return high, low


def tables():
    place = np.arange(G)
    kz = np.arange(KZ)
    m = np.arange(M)
    freq = np.where(m < M // 2, m, m - M)
    za = 2.0 * np.pi * (np.outer(kz, place) % G) / G
    fa = 2.0 * np.pi * (np.outer(place, freq) % G) / G
    c, s = np.cos(fa), np.sin(fa)
    kept = (place % 16) * 8 + place // 16
    four = np.eye(4)
    zt = np.stack([np.cos(za), -np.sin(za)], 1)[:, :, kept]
    zf_h, zf_l = split_table(np.einsum("krz,cd->krcdz", zt, four).reshape(8 * KZ, 4 * G))
    zf = np.concatenate([zf_h, zf_h, zf_l], 1)
    yf_h, yf_l = split_table(np.block([[c, -s], [s, c]]))
    yf = np.block([[yf_h, yf_l], [yf_h, np.zeros_like(yf_l)]])
    xf_h, xf_l = split_table(np.concatenate([c.T, s.T], 1))
    xf = np.concatenate([xf_h, xf_l], 0)
    xi_h, xi_l = split_table(np.concatenate([c, s], 1) / G)
    xi = np.concatenate([xi_h, xi_l], 1)
    yi_h, yi_l = split_table(np.block([[c.T, s.T], [-s.T, c.T]]) / G)
    yi = np.concatenate([yi_h, yi_h, yi_l, yi_l], 0)
    back = np.where(kz == 0, 1.0, 2.0)[:, None] / G
    zb = zt * back[:, :, None]
    zi_h, zi_l = split_table(np.einsum("krz,cd->czkrd", zb, four).reshape(4 * G, 8 * KZ))
    zi = np.concatenate([zi_h, zi_h, zi_l], 1)
    zs_h, zs_l = split_table(np.repeat(zb.transpose(2, 0, 1), NX, axis=1).reshape(G, 2 * KZ * NX))
    zs = np.concatenate([zs_h, zs_h, zs_l], 1)
    return [jnp.asarray(t, BF16) for t in (zf, yf, xf, xi, yi, zi, zs)]


def dot(a, b):
    return jnp.dot(a, b, preferred_element_type=F32)


def split(value):
    high = value.astype(BF16)
    low = (value - high.astype(F32)).astype(BF16)
    return high, low


def swap8(tiles):
    row = lax.broadcasted_iota(jnp.int32, (8, 128), 0)
    for d in (1, 2, 4):
        mask = (row // d) % 2 == 0
        new = list(tiles)
        for i in range(8):
            if i & d:
                continue
            a, b = tiles[i], tiles[i + d]
            new[i] = jnp.where(mask, a, pltpu.roll(b, d, 0))
            new[i + d] = jnp.where(mask, pltpu.roll(a, 8 - d, 0), b)
        tiles = new
    return tiles


def split3(value):
    high = value.astype(BF16)
    rest = value - high.astype(F32)
    mid = rest.astype(BF16)
    return high, mid, (rest - mid.astype(F32)).astype(BF16)


def pick(chosen, value):
    return dot(chosen, jnp.concatenate(split3(value), axis=0))


def lanes(shape):
    return lax.broadcasted_iota(jnp.int32, shape, len(shape) - 1)


def split_lanes(value):
    high = value.astype(BF16).astype(F32)
    return jnp.where(lanes(value.shape) < 64, high, value - high).astype(BF16)


def fold(value):
    return value + pltpu.roll(value, 64, 1)


def swap16(tiles):
    group = lanes(tiles[0].shape) // 8
    for d in (1, 2, 4, 8):
        mask = (group // d) % 2 == 0
        new = list(tiles)
        for i in range(16):
            if i & d:
                continue
            a, b = tiles[i], tiles[i + d]
            new[i] = jnp.where(mask, a, pltpu.roll(b, 8 * d, 1))
            new[i + d] = jnp.where(mask, pltpu.roll(a, G - 8 * d, 1), b)
        tiles = new
    return tiles


def kernel_tiles(px, py, pz):
    def local(p):
        q = p * 0.125
        return jnp.broadcast_to(q - jnp.floor(q), (8, 128))

    ux, uy, uz = local(px), local(py), local(pz)
    centre = (lax.broadcasted_iota(jnp.int32, (8, 128), 0).astype(F32) + 0.5) * 0.125
    gap = centre - uy
    base = 1.0 - gap * gap
    ex, ez = [], []
    for a in range(8):
        gx = (a + 0.5) * 0.125 - ux
        ex.append(gx * gx)
        gz = (a + 0.5) * 0.125 - uz
        ez.append(base - gz * gz)
    out = []
    for z in range(8):
        for x in range(8):
            t = jnp.maximum(ez[z] - ex[x], 0.0)
            out.append(t * t)
    return out


def points_offset(t):
    step = lax.rem(t, 4)
    return step, lax.rem(step + t // 4, 4)


def mega(
    brick, count, feat, pos, area, sdf, gain, mix, bias, spec, readout, zf_h, yf_h, xf_h, xi_h, yi_h, zi_h, zs_h,
    out,
    zf, yf, xf, xi, yi, zi, zs,
    brickv, counts, posv, areav, sdfv, gains, mixv, biases, specv, readouts,
    vecv, vecs, mixf, mixt, wbuf, homes, placed,
    sbuf, rbuf, msend, mrecv, kst, contr, g, mixed, sdft,
    send, frecv, irecv, frecv1, jsend, jrecv, plane, sacc, srow, psend, precv,
    insem, featsem, bsem, psem, msem, osem, fsem, isem, f1sem, jsem, rsem, entered,
):
    gx = lax.axis_index("gx")
    gy = lax.axis_index("gy")
    me = gx * NY + gy
    cy, core = gx // 2, lax.rem(gx, 2)
    cz, cx = gy // 4, lax.rem(gy, 4)

    def peer(dz, dx):
        return lax.rem(cz + dz, 4) * 4 + lax.rem(cx + dx, 4)

    small = [
        (brick, brickv), (count, counts), (pos, posv), (area, areav), (readout, readouts), (mix, mixv), (bias, biases),
        (gain, gains), (spec, specv), (sdf, sdfv),
        (zf_h, zf), (yf_h, yf), (xf_h, xf), (xi_h, xi), (yi_h, yi), (zi_h, zi), (zs_h, zs),
    ]
    loads = [pltpu.make_async_copy(a, b, insem.at[i]) for i, (a, b) in enumerate(small)]
    for load in loads[:4]:
        load.start()

    barrier = pltpu.get_barrier_semaphore()
    for t in range(1, NY):
        pl.semaphore_signal(barrier, inc=1, device_id=(gx, lax.rem(gy + t, NY)), device_id_type=MESH)
    for t in range(1, NX):
        pl.semaphore_signal(barrier, inc=1, device_id=(lax.rem(gx + t, NX), gy), device_id_type=MESH)

    def load_feat(n, carry):
        pltpu.make_async_copy(
            feat.at[:, pl.ds(pl.multiple_of(n * 128, 128), 128)],
            mixed.at[:, n, :], featsem,
        ).start()
        return carry

    lax.fori_loop(0, SLOTS, load_feat, 0)
    for load in loads[4:]:
        load.start()

    sub = lax.broadcasted_iota(jnp.int32, (G, G), 0)
    lane = lanes((G, G))
    one = jnp.ones((G, G), jnp.int32)
    zero = jnp.zeros((G, G), jnp.int32)

    def total(value):
        return jnp.sum(value, axis=0, keepdims=True)

    loads[0].wait()
    loads[1].wait()
    blocks = jnp.broadcast_to(brickv[...], (G, G))
    live_blocks = counts[0]
    owner = lax.shift_right_logical(blocks, 4) & 15
    inner = (lax.shift_right_logical(blocks, 8) & 1) * 16 + (blocks & 15)
    owner_t = jnp.transpose(owner)
    ahead = (owner_t == owner) & (sub < lane) & (sub < live_blocks)
    slot = jnp.where(lane[0:1] < live_blocks, owner[0:1] * CAP + total(jnp.where(ahead, one, zero)), SLOTS)
    match = jnp.where(jnp.transpose(jnp.broadcast_to(slot, (G, G))) == lane, one, zero)
    bricks = jnp.where(total(match) > 0, total(match * jnp.transpose(inner)), 32)
    msend[...] = jnp.transpose(jnp.broadcast_to(bricks, (G, G)))
    mine = pl.ds(pl.multiple_of(gy * CAP, CAP), CAP)
    mrecv[mine, :] = msend[mine, :]
    back_home = match.astype(F32).astype(BF16)
    homes[...] = jnp.concatenate([back_home] * 3, axis=1)
    to_slot = jnp.transpose(match).astype(F32).astype(BF16)
    placed[...] = jnp.concatenate([to_slot] * 3, axis=1)

    loads[2].wait()
    loads[3].wait()
    pltpu.make_async_copy(mixed, mixed, featsem).wait()

    areas = jnp.concatenate([areav[:, 128 * n : 128 * n + 128] for n in range(SLOTS)], axis=0)
    scale = pick(placed[...], areas)

    def pack(c, carry):
        h, l = split(mixed[c])
        o = dot(placed[:, 0:256], jnp.concatenate([h, l], axis=0)) * scale
        for j in range(NY):
            sbuf[j, pl.ds(pl.multiple_of(c * CAP, CAP), CAP), :] = o[CAP * j : CAP * j + CAP]
        return carry

    lax.fori_loop(0, 32, pack, 0, unroll=2)
    for k in range(3):
        o = pick(placed[...], jnp.concatenate([posv[k : k + 1, 128 * n : 128 * n + 128] for n in range(SLOTS)], axis=0))
        for j in range(NY):
            sbuf[j, 256 + 8 * k : 264 + 8 * k, :] = o[CAP * j : CAP * j + CAP]
    pl.semaphore_wait(barrier, NY + NX - 2)

    for dz, dx in POINTS[1:]:
        j = peer(dz, dx)
        pltpu.make_async_remote_copy(
            src_ref=msend.at[pl.ds(pl.multiple_of(j * CAP, CAP), CAP), :], dst_ref=mrecv.at[mine, :],
            send_sem=msem.at[0], recv_sem=msem.at[1], device_id=(gx, j), device_id_type=MESH,
        ).start()
    for dz, dx in POINTS[1:]:
        j = peer(dz, dx)
        pltpu.make_async_remote_copy(
            src_ref=sbuf.at[j], dst_ref=rbuf.at[gy],
            send_sem=bsem, recv_sem=psem.at[gy], device_id=(gx, j), device_id_type=MESH,
        ).start()
    for t in range(1, NX):
        pl.semaphore_signal(entered, inc=1, device_id=(lax.rem(gx + t, NX), gy), device_id_type=MESH)
    rbuf[gy] = sbuf[gy]

    for load in loads[4:]:
        load.wait()
    sacc[...] = jnp.transpose(sdfv[...])
    for a in range(8):
        sdft[16 * a : 16 * a + 16, :] = sacc[pl.ds(a, 16, stride=8), :]
    vec = jnp.zeros((1, 32), F32)
    shift = jnp.float32(0.0)
    for o in range(32):
        vec = vec + readouts[o] * mixv[1, o : o + 1, :]
        shift = shift + readouts[o] * biases[1, o]
    vecv[:, 0:32] = vec
    vec_copy = pltpu.make_async_copy(vecv, vecs, osem)
    vec_copy.start()
    for k in range(4):
        mixf[:, 32 * k : 32 * k + 32] = mixv[0]
    mixt[...] = split_lanes(mixf[...])
    narrow = lanes((8, 128)) < 32
    for layer in range(2):
        pair = jnp.concatenate([specv[2 * layer], specv[2 * layer + 1]], axis=0)
        for t in range(8):
            part = pair[:, 128 * t : 128 * t + 128]
            for u in range(4):
                w = jnp.where(narrow, part if u == 0 else pltpu.roll(part, G - 32 * u, 1), 0.0)
                w = w + pltpu.roll(w, 32, 1)
                wbuf[layer * 256 + (4 * t + u) * 8 : layer * 256 + (4 * t + u) * 8 + 8, :] = w + pltpu.roll(w, 64, 1)
    vec_copy.wait()

    whole = mrecv.at[pl.ds(0, (NY - 1) * CAP), :]
    pltpu.make_async_copy(whole, whole, msem.at[0]).wait()
    pltpu.make_async_copy(whole, whole, msem.at[1]).wait()
    inside = jnp.where(jnp.transpose(mrecv[...])[0:32] == sub[0:32], 1.0, 0.0).astype(BF16)
    inside = jnp.concatenate([inside, inside], axis=1)

    def encode(t, carry):
        dz, dx = points_offset(t)
        j = lax.rem(cz + 4 - dz, 4) * 4 + lax.rem(cx + 4 - dx, 4)

        @pl.when(t > 0)
        def _():
            pltpu.make_async_copy(rbuf.at[j], rbuf.at[j], psem.at[j]).wait()

        outs = []
        for i in range(CAP):
            tiles = kernel_tiles(
                rbuf[j, 256 + i : 257 + i, :], rbuf[j, 264 + i : 265 + i, :], rbuf[j, 272 + i : 273 + i, :]
            )
            kh, kl = split(jnp.concatenate(tiles, axis=0))
            fh, fl = split(rbuf[j, pl.ds(i, 32, stride=CAP), :])
            lhs = jnp.concatenate(
                [jnp.concatenate([fh, fh], axis=1), jnp.concatenate([fl, jnp.zeros_like(fl)], axis=1)], axis=0
            )
            rhs = jnp.concatenate([kh, kl], axis=1)
            kst[j * CAP + i] = rhs
            o = lax.dot_general(lhs, rhs, (((1,), (1,)), ((), ())), preferred_element_type=F32)
            outs.append(o[0:32] + o[32:64])
        for b in range(4):
            for q in range(4):
                turned = swap8([outs[i][8 * b : 8 * b + 8, 128 * q : 128 * q + 128] for i in range(CAP)])
                for i in range(CAP):
                    row = pl.multiple_of((8 * b + i) * SLOTS + j * CAP, CAP)
                    contr[q, pl.ds(row, CAP), :] = turned[i]
        return carry

    lax.fori_loop(0, NY, encode, 0)

    low = lanes((16, 128)) < 64

    def assemble(c, carry):
        for q in range(4):
            h, l = split(contr[q, pl.ds(pl.multiple_of(c * SLOTS, SLOTS), SLOTS), :])
            o = dot(inside, jnp.concatenate([h, l], axis=0))
            a, b = o[0:16], o[16:32]
            row = pl.multiple_of(c * G + 32 * q, 32)
            g[pl.ds(row, 16), :] = jnp.where(low, a, pltpu.roll(b, 64, 1))
            g[pl.ds(row + 16, 16), :] = jnp.where(low, pltpu.roll(a, 64, 1), b)
        return carry

    lax.fori_loop(0, 32, assemble, 0, unroll=2)
    pl.semaphore_wait(entered, NX - 1)

    def group_of(t):
        u = t // 2
        dy = lax.rem(2 + 3 * u + 3 * (u // 2) + 2 * (u // 3), 4)
        return lax.rem(cy + dy, 4) * 2 + lax.rem(core + 1 + lax.rem(t, 2), 2)

    partners = [peer(dz, dx) for dz, dx in FAR]

    def issue(t, grp, source_row, recv, row, size, sem):
        for n, k in enumerate(partners):
            copy = pltpu.make_async_remote_copy(
                src_ref=send.at[pl.ds(pl.multiple_of(source_row(k), size), size), :] if size == 8
                else jsend.at[pl.ds(pl.multiple_of(source_row(k), size), size), :],
                dst_ref=recv.at[pl.ds(pl.multiple_of(row, size), size), :],
                send_sem=sem.at[0], recv_sem=sem.at[1], device_id=(grp, k), device_id_type=MESH,
            )
            if n < NY - 1:
                copy.start()
            else:
                pl.when(t < NX - 1)(copy.start)

    def forward(recv, sem, prepare):
        def group(t, carry):
            grp = group_of(t)
            h, l = split(jnp.concatenate(prepare(grp), axis=0))
            rows = pl.ds(pl.multiple_of(grp * 128, 128), 128)
            send[rows, :] = dot(zf[...], jnp.concatenate([h, l, h], axis=0))
            issue(t, grp, lambda k: (grp * NY + k) * 8, recv, me * 8, 8, sem)
            return carry

        lax.fori_loop(0, NX, group, 0)
        recv[pl.ds(pl.multiple_of(me * 8, 8), 8), :] = send[pl.ds(pl.multiple_of(me * 8, 8), 8), :]

    def arrive(recv, sem, size=8):
        part = recv.at[pl.ds(0, (NX * NY - 1) * size), :]
        pltpu.make_async_copy(part, part, sem.at[1]).wait()
        pltpu.make_async_copy(part, part, sem.at[0]).wait()

    sign_f = jnp.where(lanes((1, 128)) % 64 < 32, 1.0, -1.0)

    def modes(recv, layer):
        for a in range(NX):
            tiles = [recv[(a * 16 + b) * 8 : (a * 16 + b) * 8 + 8, :] for b in range(16)]
            tiles = swap16(tiles)
            for b in range(16):
                plane[(a * 16 + b) * 8 : (a * 16 + b) * 8 + 8, :] = tiles[b]
        both = jnp.concatenate(
            [
                jnp.concatenate([plane[pl.ds(ci, G, stride=8), :], plane[pl.ds(4 + ci, G, stride=8), :]], axis=1)
                for ci in range(4)
            ],
            axis=0,
        )
        h, l = split(both)
        y = fold(dot(jnp.concatenate([h, l], axis=1), yf[...]))
        y2 = pltpu.roll(y, 96, 1) * sign_f
        r = [
            jnp.concatenate([split_lanes(y[G * ci : G * ci + G]), split_lanes(y2[G * ci : G * ci + G])], axis=0)
            for ci in range(4)
        ]
        z4 = dot(xf[...], jnp.concatenate(r, axis=1))
        z4 = z4[0:32] + z4[32:64]
        result = []
        for ci in range(4):
            z = fold(z4[:, 128 * ci : 128 * ci + 128])
            wr = wbuf[pl.ds(layer * 256 + ci, M, stride=8), :]
            wi = wbuf[pl.ds(layer * 256 + 4 + ci, M, stride=8), :]
            result.append(z * wr - pltpu.roll(z, 96, 1) * (wi * sign_f))
        return result

    def inverse_planes(parts):
        r = []
        for p in parts:
            pair = jnp.concatenate([split_lanes(p), split_lanes(pltpu.roll(p, 96, 1) * (-sign_f))], axis=0)
            r.append(jnp.concatenate([pair, pair], axis=0))
        q4 = dot(xi[...], jnp.concatenate(r, axis=1))
        q = jnp.concatenate([split_lanes(fold(q4[:, 128 * n : 128 * n + 128])) for n in range(len(parts))], axis=0)
        return dot(jnp.concatenate([q, q], axis=1), yi[...])

    def prepare0(grp):
        values = []
        for ci in range(4):
            rows = pl.ds(pl.multiple_of((grp * 4 + ci) * G, G), G)
            value = g[rows, :] + gains[grp * 4 + ci] * sdft[...]
            g[rows, :] = value
            values.append(value)
        return values

    forward(frecv, fsem, prepare0)

    mixed2 = mixed.reshape(32 * G, 128)

    def mix_cells(z, carry):
        h, l = split(g[pl.ds(z, 32, stride=G), :])
        mixed2[pl.ds(z, 32, stride=G), :] = dot(mixt[...], jnp.concatenate([h, l, h, l], axis=0))
        return carry

    lax.fori_loop(0, G, mix_cells, 0, unroll=4)
    arrive(frecv, fsem)
    o = inverse_planes(modes(frecv, 0))
    for ci in range(4):
        plane[pl.ds(ci, G, stride=8), :] = o[G * ci : G * ci + G, 0:128]
        plane[pl.ds(ci + 4, G, stride=8), :] = o[G * ci : G * ci + G, 128:256]

    spot = gy * NX + gx

    def back(t, carry):
        grp = group_of(t)
        base = pl.multiple_of(grp * 128, 128)
        tiles = swap16([plane[pl.ds(base + 8 * b, 8), :] for b in range(16)])
        for b in range(16):
            send[pl.ds(base + 8 * b, 8), :] = tiles[b]
        issue(t, grp, lambda k: (grp * NY + k) * 8, irecv, me * 8, 8, isem)
        return carry

    lax.fori_loop(0, NX, back, 0)
    irecv[pl.ds(pl.multiple_of(me * 8, 8), 8), :] = send[pl.ds(pl.multiple_of(me * 8, 8), 8), :]
    arrive(irecv, isem)
    sacc[...] = jnp.zeros_like(sacc) + shift

    def prepare1(grp):
        h, l = split(irecv[pl.ds(pl.multiple_of(grp * 128, 128), 128), :])
        spectral = dot(zi[...], jnp.concatenate([h, l, h], axis=0))
        values = []
        added = None
        for ci in range(4):
            c = grp * 4 + ci
            value = jax.nn.gelu(spectral[G * ci : G * ci + G] + mixed[c] + biases[0, c])
            added = vecs[0, c] * value if added is None else added + vecs[0, c] * value
            values.append(value)
        sacc[...] += added
        return values

    forward(frecv1, f1sem, prepare1)
    arrive(frecv1, f1sem)
    projected = None
    for ci, p in enumerate(modes(frecv1, 1)):
        p = p * readouts[gx * 4 + ci]
        projected = p if projected is None else projected + p
    o = inverse_planes([projected])
    for a in range(NX):
        for ri in range(2):
            plane[pl.ds((a // 4) * 128 + (a % 4) * 2 + ri, 16, stride=8), :] = o[16 * a : 16 * a + 16, 128 * ri : 128 * ri + 128]
    for half in range(2):
        tiles = swap16([plane[half * 128 + 8 * b : half * 128 + 8 * b + 8, :] for b in range(16)])
        for b in range(16):
            jsend[half * 128 + 8 * b : half * 128 + 8 * b + 8, :] = tiles[b]

    def back1(t, carry):
        grp = group_of(t)
        issue(t, grp, lambda k: ((grp // 4) * 16 + k) * 8 + lax.rem(grp, 4) * 2, jrecv, spot * 2, 2, jsem)
        return carry

    lax.fori_loop(0, NX, back1, 0)
    jrecv[pl.ds(pl.multiple_of(spot * 2, 2), 2), :] = jsend[
        pl.ds(pl.multiple_of(((gx // 4) * 16 + gy) * 8 + lax.rem(gx, 4) * 2, 2), 2), :
    ]
    arrive(jrecv, jsem, 2)
    h, l = split(jrecv[...])
    field = sacc[...] + dot(zs[...], jnp.concatenate([h, l, h], axis=0))

    left = lanes((16, 128)) < 64
    for q in range(4):
        a = field[32 * q : 32 * q + 16]
        b = field[32 * q + 16 : 32 * q + 32]
        for bx in range(2):
            w = jnp.where(left, a, pltpu.roll(b, 64, 1)) if bx == 0 else jnp.where(left, pltpu.roll(a, 64, 1), b)
            h, l = split(w)
            srow[16 * bx : 16 * bx + 16, 128 * q : 128 * q + 128] = h
            srow[32 + 16 * bx : 48 + 16 * bx, 128 * q : 128 * q + 128] = l
    srow[64:80, :] = jnp.ones((16, 512), BF16)
    which = sub[0:32]

    def decode(j, carry):
        nums, dens = [], []
        for i in range(CAP):
            o = dot(srow[...], kst[j * CAP + i])
            o = o[0:72, 0:128] + o[0:72, 128:256]
            owned = jnp.broadcast_to(mrecv[pl.ds(j * CAP + i, 1), :], (32, 128)) == which
            nums.append(total(jnp.where(owned, o[0:32] + o[32:64], 0.0)))
            dens.append(o[64:65])
        psend[pl.ds(pl.multiple_of(j * CAP, CAP), CAP), :] = jnp.concatenate(nums, axis=0) / jnp.concatenate(dens, axis=0)
        return carry

    lax.fori_loop(0, NY, decode, 0)
    precv[mine, :] = psend[mine, :]
    for dz, dx in FAR[:-1]:
        j = peer(dz, dx)
        pltpu.make_async_remote_copy(
            src_ref=psend.at[pl.ds(pl.multiple_of(j * CAP, CAP), CAP), :], dst_ref=precv.at[mine, :],
            send_sem=rsem.at[0], recv_sem=rsem.at[1], device_id=(gx, j), device_id_type=MESH,
        ).start()
    part = precv.at[pl.ds(0, (NY - 1) * CAP), :]
    pltpu.make_async_copy(part, part, rsem.at[1]).wait()
    pltpu.make_async_copy(part, part, rsem.at[0]).wait()
    sent = sbuf.at[pl.ds(0, NY - 1)]
    pltpu.make_async_copy(sent, sent, bsem).wait()

    out[...] = pick(homes[...], precv[...])


def per_device(positions, point_feat, area, block_brick, block_count, sdf, grid_gain, mix_w, mix_b, spec_w, readout_w):
    consts = tables()
    hbm = pl.BlockSpec(memory_space=pl.ANY)
    dma = pltpu.SemaphoreType.DMA
    vmem = pltpu.VMEM
    i32 = jnp.int32
    out = pl.pallas_call(
        mega,
        out_shape=jax.ShapeDtypeStruct((SLOTS, 128), F32),
        in_specs=[hbm] * (11 + len(consts)),
        out_specs=pl.BlockSpec(memory_space=vmem),
        scratch_shapes=[vmem(t.shape, BF16) for t in consts]
        + [
            vmem((1, SLOTS), i32),
            pltpu.SMEM((1,), i32),
            vmem((3, SLOTS * 128), F32),
            vmem((1, SLOTS * 128), F32),
            vmem((G, 128), F32),
            pltpu.SMEM((32,), F32),
            vmem((2, 32, 32), F32),
            pltpu.SMEM((2, 32), F32),
            vmem((4, 4, M * M), F32),
            pltpu.SMEM((32,), F32),
            vmem((1, 128), F32),
            pltpu.SMEM((1, 128), F32),
            vmem((32, 128), F32),
            vmem((32, 128), BF16),
            vmem((512, 128), F32),
            vmem((SLOTS, 384), BF16),
            vmem((SLOTS, 384), BF16),
            vmem((NY, ROWS, 128), F32),
            vmem((NY, ROWS, 128), F32),
            vmem((SLOTS, 128), i32),
            vmem((SLOTS, 128), i32),
            vmem((SLOTS, 512, 256), BF16),
            vmem((4, SLOTS * 32, 128), F32),
            vmem((32 * G, 128), F32),
            vmem((32, G, 128), F32),
            vmem((G, 128), F32),
            vmem((1024, 128), F32),
            vmem((1024, 128), F32),
            vmem((1024, 128), F32),
            vmem((1024, 128), F32),
            vmem((256, 128), F32),
            vmem((256, 128), F32),
            vmem((1024, 128), F32),
            vmem((G, 128), F32),
            vmem((80, 512), BF16),
            vmem((SLOTS, 128), F32),
            vmem((SLOTS, 128), F32),
            dma((10 + len(consts),)), dma, dma, dma((NY,)), dma((2,)), dma, dma((2,)), dma((2,)), dma((2,)),
            dma((2,)), dma((2,)), pltpu.SemaphoreType.REGULAR,
        ],
        compiler_params=pltpu.CompilerParams(collective_id=0, has_side_effects=True, vmem_limit_bytes=67043328),
        name="operator",
    )(
        block_brick.reshape(1, SLOTS), block_count, point_feat, positions, area.reshape(1, SLOTS * 128), sdf.reshape(G, 128),
        grid_gain, mix_w, mix_b, spec_w.reshape(4, 4, M * M), readout_w, *consts,
    )
    return out.reshape(SLOTS * 128)


def solution(mesh):
    placed = (
        P(None, ("gx", "gy")),
        P(None, ("gx", "gy")),
        P(("gx", "gy")),
        P(("gx", "gy")),
        P(("gx", "gy")),
        P("gx", "gy", None),
        P(),
        P(),
        P(),
        P(None, None, "gy", "gx", None),
        P(),
    )
    return jax.shard_map(per_device, mesh=mesh, in_specs=placed, out_specs=P(("gx", "gy")), check_vma=False)
```

```python
import functools

import jax
import jax.numpy as jnp
import ml_dtypes
import numpy as np
from jax import lax
from jax.experimental import pallas as pl
from jax.experimental.pallas import tpu as pltpu
from jax.sharding import PartitionSpec as P

MESH = pl.DeviceIdType.MESH
F32 = jnp.float32
BF16 = jnp.bfloat16

G = 128
M = 32
KZ = 16
NX = 8
NY = 16
CAP = 8
SLOTS = NY * CAP
ROWS = CAP * 32 + 3 * CAP
POINTS = [(t % 4, (t % 4 + t // 4) % 4) for t in range(16)]
FAR = [(2, 2), (2, 1), (1, 2), (2, 3), (3, 2), (1, 1), (3, 3), (3, 1), (1, 3), (2, 0), (0, 2), (0, 1), (1, 0), (0, 3), (3, 0), (0, 0)]


def split_table(table):
    high = table.astype(ml_dtypes.bfloat16)
    low = (table - high.astype(np.float64)).astype(ml_dtypes.bfloat16)
    return high, low


def tables():
    place = np.arange(G)
    kz = np.arange(KZ)
    m = np.arange(M)
    freq = np.where(m < M // 2, m, m - M)
    za = 2.0 * np.pi * (np.outer(kz, place) % G) / G
    fa = 2.0 * np.pi * (np.outer(place, freq) % G) / G
    c, s = np.cos(fa), np.sin(fa)
    kept = (place % 16) * 8 + place // 16
    four = np.eye(4)
    zt = np.stack([np.cos(za), -np.sin(za)], 1)[:, :, kept]
    zf_h, zf_l = split_table(np.einsum("krz,cd->krcdz", zt, four).reshape(8 * KZ, 4 * G))
    zf = np.concatenate([zf_h, zf_h, zf_l], 1)
    yf_h, yf_l = split_table(np.block([[c, -s], [s, c]]))
    yf = np.block([[yf_h, yf_l], [yf_h, np.zeros_like(yf_l)]])
    xf_h, xf_l = split_table(np.concatenate([c.T, s.T], 1))
    xf = np.concatenate([xf_h, xf_l], 0)
    xi_h, xi_l = split_table(np.concatenate([c, s], 1) / G)
    xi = np.concatenate([xi_h, xi_l], 1)
    yi_h, yi_l = split_table(np.block([[c.T, s.T], [-s.T, c.T]]) / G)
    yi = np.concatenate([yi_h, yi_h, yi_l, yi_l], 0)
    back = np.where(kz == 0, 1.0, 2.0)[:, None] / G
    zb = zt * back[:, :, None]
    zi_h, zi_l = split_table(np.einsum("krz,cd->czkrd", zb, four).reshape(4 * G, 8 * KZ))
    zi = np.concatenate([zi_h, zi_h, zi_l], 1)
    zs_h, zs_l = split_table(np.repeat(zb.transpose(2, 0, 1), NX, axis=1).reshape(G, 2 * KZ * NX))
    zs = np.concatenate([zs_h, zs_h, zs_l], 1)
    return [jnp.asarray(t, BF16) for t in (zf, yf, xf, xi, yi, zi, zs)]


def dot(a, b):
    return jnp.dot(a, b, preferred_element_type=F32)


def split(value):
    high = value.astype(BF16)
    low = (value - high.astype(F32)).astype(BF16)
    return high, low


def swap8(tiles):
    row = lax.broadcasted_iota(jnp.int32, (8, 128), 0)
    for d in (1, 2, 4):
        mask = (row // d) % 2 == 0
        new = list(tiles)
        for i in range(8):
            if i & d:
                continue
            a, b = tiles[i], tiles[i + d]
            new[i] = jnp.where(mask, a, pltpu.roll(b, d, 0))
            new[i + d] = jnp.where(mask, pltpu.roll(a, 8 - d, 0), b)
        tiles = new
    return tiles


def split3(value):
    high = value.astype(BF16)
    rest = value - high.astype(F32)
    mid = rest.astype(BF16)
    return high, mid, (rest - mid.astype(F32)).astype(BF16)


def pick(chosen, value):
    return dot(chosen, jnp.concatenate(split3(value), axis=0))


def lanes(shape):
    return lax.broadcasted_iota(jnp.int32, shape, len(shape) - 1)


def split_lanes(value):
    high = value.astype(BF16).astype(F32)
    return jnp.where(lanes(value.shape) < 64, high, value - high).astype(BF16)


def fold(value):
    return value + pltpu.roll(value, 64, 1)


def swap16(tiles):
    group = lanes(tiles[0].shape) // 8
    for d in (1, 2, 4, 8):
        mask = (group // d) % 2 == 0
        new = list(tiles)
        for i in range(16):
            if i & d:
                continue
            a, b = tiles[i], tiles[i + d]
            new[i] = jnp.where(mask, a, pltpu.roll(b, 8 * d, 1))
            new[i + d] = jnp.where(mask, pltpu.roll(a, G - 8 * d, 1), b)
        tiles = new
    return tiles


def kernel_tiles(px, py, pz):
    def local(p):
        q = p * 0.125
        return jnp.broadcast_to(q - jnp.floor(q), (8, 128))

    ux, uy, uz = local(px), local(py), local(pz)
    centre = (lax.broadcasted_iota(jnp.int32, (8, 128), 0).astype(F32) + 0.5) * 0.125
    gap = centre - uy
    base = 1.0 - gap * gap
    ex, ez = [], []
    for a in range(8):
        gx = (a + 0.5) * 0.125 - ux
        ex.append(gx * gx)
        gz = (a + 0.5) * 0.125 - uz
        ez.append(base - gz * gz)
    out = []
    for z in range(8):
        for x in range(8):
            t = jnp.maximum(ez[z] - ex[x], 0.0)
            out.append(t * t)
    return out


def points_offset(t):
    step = lax.rem(t, 4)
    return step, lax.rem(step + t // 4, 4)


def mega(
    brick, count, feat, pos, area, sdf, gain, mix, bias, spec, readout, zf_h, yf_h, xf_h, xi_h, yi_h, zi_h, zs_h,
    out,
    zf, yf, xf, xi, yi, zi, zs,
    brickv, counts, posv, areav, sdfv, gains, mixv, biases, specv, readouts,
    vecv, vecs, mixf, mixt, wbuf, homes, placed,
    sbuf, rbuf, msend, mrecv, kst, contr, g, mixed, sdft,
    send, frecv, irecv, frecv1, jsend, jrecv, plane, sacc, srow, psend, precv,
    insem, featsem, bsem, psem, msem, osem, fsem, isem, f1sem, jsem, rsem, entered,
):
    gx = lax.axis_index("gx")
    gy = lax.axis_index("gy")
    me = gx * NY + gy
    cy, core = gx // 2, lax.rem(gx, 2)
    cz, cx = gy // 4, lax.rem(gy, 4)

    def peer(dz, dx):
        return lax.rem(cz + dz, 4) * 4 + lax.rem(cx + dx, 4)

    small = [
        (brick, brickv), (count, counts), (pos, posv), (area, areav), (readout, readouts), (mix, mixv), (bias, biases),
        (gain, gains), (spec, specv), (sdf, sdfv),
        (zf_h, zf), (yf_h, yf), (xf_h, xf), (xi_h, xi), (yi_h, yi), (zi_h, zi), (zs_h, zs),
    ]
    loads = [pltpu.make_async_copy(a, b, insem.at[i]) for i, (a, b) in enumerate(small)]
    for load in loads[:4]:
        load.start()

    barrier = pltpu.get_barrier_semaphore()
    for t in range(1, NY):
        pl.semaphore_signal(barrier, inc=1, device_id=(gx, lax.rem(gy + t, NY)), device_id_type=MESH)
    for t in range(1, NX):
        pl.semaphore_signal(barrier, inc=1, device_id=(lax.rem(gx + t, NX), gy), device_id_type=MESH)

    def load_feat(n, carry):
        pltpu.make_async_copy(
            feat.at[:, pl.ds(pl.multiple_of(n * 128, 128), 128)],
            mixed.at[:, n, :], featsem,
        ).start()
        return carry

    lax.fori_loop(0, SLOTS, load_feat, 0)
    for load in loads[4:]:
        load.start()

    sub = lax.broadcasted_iota(jnp.int32, (G, G), 0)
    lane = lanes((G, G))
    one = jnp.ones((G, G), jnp.int32)
    zero = jnp.zeros((G, G), jnp.int32)

    def total(value):
        return jnp.sum(value, axis=0, keepdims=True)

    loads[0].wait()
    loads[1].wait()
    blocks = jnp.broadcast_to(brickv[...], (G, G))
    live_blocks = counts[0]
    owner = lax.shift_right_logical(blocks, 4) & 15
    inner = (lax.shift_right_logical(blocks, 8) & 1) * 16 + (blocks & 15)
    owner_t = jnp.transpose(owner)
    ahead = (owner_t == owner) & (sub < lane) & (sub < live_blocks)
    slot = jnp.where(lane[0:1] < live_blocks, owner[0:1] * CAP + total(jnp.where(ahead, one, zero)), SLOTS)
    match = jnp.where(jnp.transpose(jnp.broadcast_to(slot, (G, G))) == lane, one, zero)
    bricks = jnp.where(total(match) > 0, total(match * jnp.transpose(inner)), 32)
    msend[...] = jnp.transpose(jnp.broadcast_to(bricks, (G, G)))
    mine = pl.ds(pl.multiple_of(gy * CAP, CAP), CAP)
    mrecv[mine, :] = msend[mine, :]
    back_home = match.astype(F32).astype(BF16)
    homes[...] = jnp.concatenate([back_home] * 3, axis=1)
    to_slot = jnp.transpose(match).astype(F32).astype(BF16)
    placed[...] = jnp.concatenate([to_slot] * 3, axis=1)

    loads[2].wait()
    loads[3].wait()
    pltpu.make_async_copy(mixed, mixed, featsem).wait()

    areas = jnp.concatenate([areav[:, 128 * n : 128 * n + 128] for n in range(SLOTS)], axis=0)
    scale = pick(placed[...], areas)

    def pack(c, carry):
        h, l = split(mixed[c])
        o = dot(placed[:, 0:256], jnp.concatenate([h, l], axis=0)) * scale
        for j in range(NY):
            sbuf[j, pl.ds(pl.multiple_of(c * CAP, CAP), CAP), :] = o[CAP * j : CAP * j + CAP]
        return carry

    lax.fori_loop(0, 32, pack, 0, unroll=2)
    for k in range(3):
        o = pick(placed[...], jnp.concatenate([posv[k : k + 1, 128 * n : 128 * n + 128] for n in range(SLOTS)], axis=0))
        for j in range(NY):
            sbuf[j, 256 + 8 * k : 264 + 8 * k, :] = o[CAP * j : CAP * j + CAP]
    pl.semaphore_wait(barrier, NY + NX - 2)

    for dz, dx in POINTS[1:]:
        j = peer(dz, dx)
        pltpu.make_async_remote_copy(
            src_ref=msend.at[pl.ds(pl.multiple_of(j * CAP, CAP), CAP), :], dst_ref=mrecv.at[mine, :],
            send_sem=msem.at[0], recv_sem=msem.at[1], device_id=(gx, j), device_id_type=MESH,
        ).start()
    for dz, dx in POINTS[1:]:
        j = peer(dz, dx)
        pltpu.make_async_remote_copy(
            src_ref=sbuf.at[j], dst_ref=rbuf.at[gy],
            send_sem=bsem, recv_sem=psem.at[gy], device_id=(gx, j), device_id_type=MESH,
        ).start()
    for t in range(1, NX):
        pl.semaphore_signal(entered, inc=1, device_id=(lax.rem(gx + t, NX), gy), device_id_type=MESH)
    rbuf[gy] = sbuf[gy]

    for load in loads[4:]:
        load.wait()
    sacc[...] = jnp.transpose(sdfv[...])
    for a in range(8):
        sdft[16 * a : 16 * a + 16, :] = sacc[pl.ds(a, 16, stride=8), :]
    vec = jnp.zeros((1, 32), F32)
    shift = jnp.float32(0.0)
    for o in range(32):
        vec = vec + readouts[o] * mixv[1, o : o + 1, :]
        shift = shift + readouts[o] * biases[1, o]
    vecv[:, 0:32] = vec
    vec_copy = pltpu.make_async_copy(vecv, vecs, osem)
    vec_copy.start()
    for k in range(4):
        mixf[:, 32 * k : 32 * k + 32] = mixv[0]
    mixt[...] = split_lanes(mixf[...])
    narrow = lanes((8, 128)) < 32
    for layer in range(2):
        pair = jnp.concatenate([specv[2 * layer], specv[2 * layer + 1]], axis=0)
        for t in range(8):
            part = pair[:, 128 * t : 128 * t + 128]
            for u in range(4):
                w = jnp.where(narrow, part if u == 0 else pltpu.roll(part, G - 32 * u, 1), 0.0)
                w = w + pltpu.roll(w, 32, 1)
                wbuf[layer * 256 + (4 * t + u) * 8 : layer * 256 + (4 * t + u) * 8 + 8, :] = w + pltpu.roll(w, 64, 1)
    vec_copy.wait()

    whole = mrecv.at[pl.ds(0, (NY - 1) * CAP), :]
    pltpu.make_async_copy(whole, whole, msem.at[0]).wait()
    pltpu.make_async_copy(whole, whole, msem.at[1]).wait()
    inside = jnp.where(jnp.transpose(mrecv[...])[0:32] == sub[0:32], 1.0, 0.0).astype(BF16)
    inside = jnp.concatenate([inside, inside], axis=1)

    def encode(t, carry):
        dz, dx = points_offset(t)
        j = lax.rem(cz + 4 - dz, 4) * 4 + lax.rem(cx + 4 - dx, 4)

        @pl.when(t > 0)
        def _():
            pltpu.make_async_copy(rbuf.at[j], rbuf.at[j], psem.at[j]).wait()

        outs = []
        for i in range(CAP):
            tiles = kernel_tiles(
                rbuf[j, 256 + i : 257 + i, :], rbuf[j, 264 + i : 265 + i, :], rbuf[j, 272 + i : 273 + i, :]
            )
            kh, kl = split(jnp.concatenate(tiles, axis=0))
            fh, fl = split(rbuf[j, pl.ds(i, 32, stride=CAP), :])
            lhs = jnp.concatenate(
                [jnp.concatenate([fh, fh], axis=1), jnp.concatenate([fl, jnp.zeros_like(fl)], axis=1)], axis=0
            )
            rhs = jnp.concatenate([kh, kl], axis=1)
            kst[j * CAP + i] = rhs
            o = lax.dot_general(lhs, rhs, (((1,), (1,)), ((), ())), preferred_element_type=F32)
            outs.append(o[0:32] + o[32:64])
        for b in range(4):
            for q in range(4):
                turned = swap8([outs[i][8 * b : 8 * b + 8, 128 * q : 128 * q + 128] for i in range(CAP)])
                for i in range(CAP):
                    row = pl.multiple_of((8 * b + i) * SLOTS + j * CAP, CAP)
                    contr[q, pl.ds(row, CAP), :] = turned[i]
        return carry

    lax.fori_loop(0, NY, encode, 0)

    low = lanes((16, 128)) < 64
    pl.semaphore_wait(entered, NX - 1)

    def group_of(t):
        u = t // 2
        dy = lax.rem(2 + 3 * u + 3 * (u // 2) + 2 * (u // 3), 4)
        return lax.rem(cy + dy, 4) * 2 + lax.rem(core + 1 + lax.rem(t, 2), 2)

    partners = [peer(dz, dx) for dz, dx in FAR]

    def issue(t, grp, source_row, recv, row, size, sem):
        for n, k in enumerate(partners):
            copy = pltpu.make_async_remote_copy(
                src_ref=send.at[pl.ds(pl.multiple_of(source_row(k), size), size), :] if size == 8
                else jsend.at[pl.ds(pl.multiple_of(source_row(k), size), size), :],
                dst_ref=recv.at[pl.ds(pl.multiple_of(row, size), size), :],
                send_sem=sem.at[0], recv_sem=sem.at[1], device_id=(grp, k), device_id_type=MESH,
            )
            if n < NY - 1:
                copy.start()
            else:
                pl.when(t < NX - 1)(copy.start)

    def forward(recv, sem, prepare):
        def group(t, carry):
            grp = group_of(t)
            h, l = split(jnp.concatenate(prepare(grp), axis=0))
            rows = pl.ds(pl.multiple_of(grp * 128, 128), 128)
            send[rows, :] = dot(zf[...], jnp.concatenate([h, l, h], axis=0))
            issue(t, grp, lambda k: (grp * NY + k) * 8, recv, me * 8, 8, sem)
            return carry

        lax.fori_loop(0, NX, group, 0)
        recv[pl.ds(pl.multiple_of(me * 8, 8), 8), :] = send[pl.ds(pl.multiple_of(me * 8, 8), 8), :]

    def arrive(recv, sem, size=8):
        part = recv.at[pl.ds(0, (NX * NY - 1) * size), :]
        pltpu.make_async_copy(part, part, sem.at[1]).wait()
        pltpu.make_async_copy(part, part, sem.at[0]).wait()

    sign_f = jnp.where(lanes((1, 128)) % 64 < 32, 1.0, -1.0)

    def modes(recv, layer):
        for a in range(NX):
            tiles = [recv[(a * 16 + b) * 8 : (a * 16 + b) * 8 + 8, :] for b in range(16)]
            tiles = swap16(tiles)
            for b in range(16):
                plane[(a * 16 + b) * 8 : (a * 16 + b) * 8 + 8, :] = tiles[b]
        both = jnp.concatenate(
            [
                jnp.concatenate([plane[pl.ds(ci, G, stride=8), :], plane[pl.ds(4 + ci, G, stride=8), :]], axis=1)
                for ci in range(4)
            ],
            axis=0,
        )
        h, l = split(both)
        y = fold(dot(jnp.concatenate([h, l], axis=1), yf[...]))
        y2 = pltpu.roll(y, 96, 1) * sign_f
        r = [
            jnp.concatenate([split_lanes(y[G * ci : G * ci + G]), split_lanes(y2[G * ci : G * ci + G])], axis=0)
            for ci in range(4)
        ]
        z4 = dot(xf[...], jnp.concatenate(r, axis=1))
        z4 = z4[0:32] + z4[32:64]
        result = []
        for ci in range(4):
            z = fold(z4[:, 128 * ci : 128 * ci + 128])
            wr = wbuf[pl.ds(layer * 256 + ci, M, stride=8), :]
            wi = wbuf[pl.ds(layer * 256 + 4 + ci, M, stride=8), :]
            result.append(z * wr - pltpu.roll(z, 96, 1) * (wi * sign_f))
        return result

    def inverse_planes(parts):
        r = []
        for p in parts:
            pair = jnp.concatenate([split_lanes(p), split_lanes(pltpu.roll(p, 96, 1) * (-sign_f))], axis=0)
            r.append(jnp.concatenate([pair, pair], axis=0))
        q4 = dot(xi[...], jnp.concatenate(r, axis=1))
        q = jnp.concatenate([split_lanes(fold(q4[:, 128 * n : 128 * n + 128])) for n in range(len(parts))], axis=0)
        return dot(jnp.concatenate([q, q], axis=1), yi[...])

    def prepare0(grp):
        values = []
        for ci in range(4):
            c = grp * 4 + ci
            pieces = []
            for q in range(4):
                h, l = split(contr[q, pl.ds(pl.multiple_of(c * SLOTS, SLOTS), SLOTS), :])
                o = dot(inside, jnp.concatenate([h, l], axis=0))
                a, b = o[0:16], o[16:32]
                pieces.append(jnp.where(low, a, pltpu.roll(b, 64, 1)))
                pieces.append(jnp.where(low, pltpu.roll(a, 64, 1), b))
            value = jnp.concatenate(pieces, axis=0) + gains[c] * sdft[...]
            g[pl.ds(pl.multiple_of(c * G, G), G), :] = value
            values.append(value)
        return values

    forward(frecv, fsem, prepare0)

    mixed2 = mixed.reshape(32 * G, 128)

    def mix_cells(z, carry):
        h, l = split(g[pl.ds(z, 32, stride=G), :])
        mixed2[pl.ds(z, 32, stride=G), :] = dot(mixt[...], jnp.concatenate([h, l, h, l], axis=0))
        return carry

    lax.fori_loop(0, G // 2, mix_cells, 0, unroll=4)
    arrive(frecv, fsem)
    o = inverse_planes(modes(frecv, 0))
    for ci in range(4):
        plane[pl.ds(ci, G, stride=8), :] = o[G * ci : G * ci + G, 0:128]
        plane[pl.ds(ci + 4, G, stride=8), :] = o[G * ci : G * ci + G, 128:256]

    spot = gy * NX + gx

    def back(t, carry):
        grp = group_of(t)
        base = pl.multiple_of(grp * 128, 128)
        tiles = swap16([plane[pl.ds(base + 8 * b, 8), :] for b in range(16)])
        for b in range(16):
            send[pl.ds(base + 8 * b, 8), :] = tiles[b]
        issue(t, grp, lambda k: (grp * NY + k) * 8, irecv, me * 8, 8, isem)
        return carry

    lax.fori_loop(0, NX, back, 0)
    irecv[pl.ds(pl.multiple_of(me * 8, 8), 8), :] = send[pl.ds(pl.multiple_of(me * 8, 8), 8), :]
    lax.fori_loop(G // 2, G, mix_cells, 0, unroll=4)
    arrive(irecv, isem)
    sacc[...] = jnp.zeros_like(sacc) + shift

    def prepare1(grp):
        h, l = split(irecv[pl.ds(pl.multiple_of(grp * 128, 128), 128), :])
        spectral = dot(zi[...], jnp.concatenate([h, l, h], axis=0))
        values = []
        added = None
        for ci in range(4):
            c = grp * 4 + ci
            value = jax.nn.gelu(spectral[G * ci : G * ci + G] + mixed[c] + biases[0, c])
            added = vecs[0, c] * value if added is None else added + vecs[0, c] * value
            values.append(value)
        sacc[...] += added
        return values

    forward(frecv1, f1sem, prepare1)
    arrive(frecv1, f1sem)
    projected = None
    for ci, p in enumerate(modes(frecv1, 1)):
        p = p * readouts[gx * 4 + ci]
        projected = p if projected is None else projected + p
    o = inverse_planes([projected])
    for a in range(NX):
        for ri in range(2):
            plane[pl.ds((a // 4) * 128 + (a % 4) * 2 + ri, 16, stride=8), :] = o[16 * a : 16 * a + 16, 128 * ri : 128 * ri + 128]
    for half in range(2):
        tiles = swap16([plane[half * 128 + 8 * b : half * 128 + 8 * b + 8, :] for b in range(16)])
        for b in range(16):
            jsend[half * 128 + 8 * b : half * 128 + 8 * b + 8, :] = tiles[b]

    def back1(t, carry):
        grp = group_of(t)
        issue(t, grp, lambda k: ((grp // 4) * 16 + k) * 8 + lax.rem(grp, 4) * 2, jrecv, spot * 2, 2, jsem)
        return carry

    lax.fori_loop(0, NX, back1, 0)
    jrecv[pl.ds(pl.multiple_of(spot * 2, 2), 2), :] = jsend[
        pl.ds(pl.multiple_of(((gx // 4) * 16 + gy) * 8 + lax.rem(gx, 4) * 2, 2), 2), :
    ]
    arrive(jrecv, jsem, 2)
    h, l = split(jrecv[...])
    field = sacc[...] + dot(zs[...], jnp.concatenate([h, l, h], axis=0))

    left = lanes((16, 128)) < 64
    for q in range(4):
        a = field[32 * q : 32 * q + 16]
        b = field[32 * q + 16 : 32 * q + 32]
        for bx in range(2):
            w = jnp.where(left, a, pltpu.roll(b, 64, 1)) if bx == 0 else jnp.where(left, pltpu.roll(a, 64, 1), b)
            h, l = split(w)
            srow[16 * bx : 16 * bx + 16, 128 * q : 128 * q + 128] = h
            srow[32 + 16 * bx : 48 + 16 * bx, 128 * q : 128 * q + 128] = l
    srow[64:80, :] = jnp.ones((16, 512), BF16)
    which = sub[0:32]

    def decode(u, carry):
        dz, dx = points_offset(NY - 1 - u)
        j = peer(dz, dx)
        nums, dens = [], []
        for i in range(CAP):
            o = dot(srow[...], kst[j * CAP + i])
            o = o[0:72, 0:128] + o[0:72, 128:256]
            owned = jnp.broadcast_to(mrecv[pl.ds(j * CAP + i, 1), :], (32, 128)) == which
            nums.append(total(jnp.where(owned, o[0:32] + o[32:64], 0.0)))
            dens.append(o[64:65])
        psend[pl.ds(pl.multiple_of(j * CAP, CAP), CAP), :] = jnp.concatenate(nums, axis=0) / jnp.concatenate(dens, axis=0)

        @pl.when(u < NY - 1)
        def _():
            pltpu.make_async_remote_copy(
                src_ref=psend.at[pl.ds(pl.multiple_of(j * CAP, CAP), CAP), :], dst_ref=precv.at[mine, :],
                send_sem=rsem.at[0], recv_sem=rsem.at[1], device_id=(gx, j), device_id_type=MESH,
            ).start()

        return carry

    lax.fori_loop(0, NY, decode, 0)
    precv[mine, :] = psend[mine, :]
    part = precv.at[pl.ds(0, (NY - 1) * CAP), :]
    pltpu.make_async_copy(part, part, rsem.at[1]).wait()
    pltpu.make_async_copy(part, part, rsem.at[0]).wait()
    sent = sbuf.at[pl.ds(0, NY - 1)]
    pltpu.make_async_copy(sent, sent, bsem).wait()

    out[...] = pick(homes[...], precv[...])


def per_device(positions, point_feat, area, block_brick, block_count, sdf, grid_gain, mix_w, mix_b, spec_w, readout_w):
    consts = tables()
    hbm = pl.BlockSpec(memory_space=pl.ANY)
    dma = pltpu.SemaphoreType.DMA
    vmem = pltpu.VMEM
    i32 = jnp.int32
    out = pl.pallas_call(
        mega,
        out_shape=jax.ShapeDtypeStruct((SLOTS, 128), F32),
        in_specs=[hbm] * (11 + len(consts)),
        out_specs=pl.BlockSpec(memory_space=vmem),
        scratch_shapes=[vmem(t.shape, BF16) for t in consts]
        + [
            vmem((1, SLOTS), i32),
            pltpu.SMEM((1,), i32),
            vmem((3, SLOTS * 128), F32),
            vmem((1, SLOTS * 128), F32),
            vmem((G, 128), F32),
            pltpu.SMEM((32,), F32),
            vmem((2, 32, 32), F32),
            pltpu.SMEM((2, 32), F32),
            vmem((4, 4, M * M), F32),
            pltpu.SMEM((32,), F32),
            vmem((1, 128), F32),
            pltpu.SMEM((1, 128), F32),
            vmem((32, 128), F32),
            vmem((32, 128), BF16),
            vmem((512, 128), F32),
            vmem((SLOTS, 384), BF16),
            vmem((SLOTS, 384), BF16),
            vmem((NY, ROWS, 128), F32),
            vmem((NY, ROWS, 128), F32),
            vmem((SLOTS, 128), i32),
            vmem((SLOTS, 128), i32),
            vmem((SLOTS, 512, 256), BF16),
            vmem((4, SLOTS * 32, 128), F32),
            vmem((32 * G, 128), F32),
            vmem((32, G, 128), F32),
            vmem((G, 128), F32),
            vmem((1024, 128), F32),
            vmem((1024, 128), F32),
            vmem((1024, 128), F32),
            vmem((1024, 128), F32),
            vmem((256, 128), F32),
            vmem((256, 128), F32),
            vmem((1024, 128), F32),
            vmem((G, 128), F32),
            vmem((80, 512), BF16),
            vmem((SLOTS, 128), F32),
            vmem((SLOTS, 128), F32),
            dma((10 + len(consts),)), dma, dma, dma((NY,)), dma((2,)), dma, dma((2,)), dma((2,)), dma((2,)),
            dma((2,)), dma((2,)), pltpu.SemaphoreType.REGULAR,
        ],
        compiler_params=pltpu.CompilerParams(collective_id=0, has_side_effects=True, vmem_limit_bytes=67043328),
        name="operator",
    )(
        block_brick.reshape(1, SLOTS), block_count, point_feat, positions, area.reshape(1, SLOTS * 128), sdf.reshape(G, 128),
        grid_gain, mix_w, mix_b, spec_w.reshape(4, 4, M * M), readout_w, *consts,
    )
    return out.reshape(SLOTS * 128)


def solution(mesh):
    placed = (
        P(None, ("gx", "gy")),
        P(None, ("gx", "gy")),
        P(("gx", "gy")),
        P(("gx", "gy")),
        P(("gx", "gy")),
        P("gx", "gy", None),
        P(),
        P(),
        P(),
        P(None, None, "gy", "gx", None),
        P(),
    )
    return jax.shard_map(per_device, mesh=mesh, in_specs=placed, out_specs=P(("gx", "gy")), check_vma=False)
```

```python
import functools

import jax
import jax.numpy as jnp
import ml_dtypes
import numpy as np
from jax import lax
from jax.experimental import pallas as pl
from jax.experimental.pallas import tpu as pltpu
from jax.sharding import PartitionSpec as P

MESH = pl.DeviceIdType.MESH
F32 = jnp.float32
BF16 = jnp.bfloat16

G = 128
M = 32
KZ = 16
NX = 8
NY = 16
CAP = 8
SLOTS = NY * CAP
ROWS = CAP * 32 + 3 * CAP
POINTS = [(t % 4, (t % 4 + t // 4) % 4) for t in range(16)]
FAR = [(2, 2), (2, 1), (1, 2), (2, 3), (3, 2), (1, 1), (3, 3), (3, 1), (1, 3), (2, 0), (0, 2), (0, 1), (1, 0), (0, 3), (3, 0), (0, 0)]


def split_table(table):
    high = table.astype(ml_dtypes.bfloat16)
    low = (table - high.astype(np.float64)).astype(ml_dtypes.bfloat16)
    return high, low


def tables():
    place = np.arange(G)
    kz = np.arange(KZ)
    m = np.arange(M)
    freq = np.where(m < M // 2, m, m - M)
    za = 2.0 * np.pi * (np.outer(kz, place) % G) / G
    fa = 2.0 * np.pi * (np.outer(place, freq) % G) / G
    c, s = np.cos(fa), np.sin(fa)
    kept = (place % 16) * 8 + place // 16
    four = np.eye(4)
    zt = np.stack([np.cos(za), -np.sin(za)], 1)[:, :, kept]
    zf_h, zf_l = split_table(np.einsum("krz,cd->krcdz", zt, four).reshape(8 * KZ, 4 * G))
    zf = np.concatenate([zf_h, zf_h, zf_l], 1)
    yf_h, yf_l = split_table(np.block([[c, -s], [s, c]]))
    yf = np.block([[yf_h, yf_l], [yf_h, np.zeros_like(yf_l)]])
    xf_h, xf_l = split_table(np.concatenate([c.T, s.T], 1))
    xf = np.concatenate([xf_h, xf_l], 0)
    xi_h, xi_l = split_table(np.concatenate([c, s], 1) / G)
    xi = np.concatenate([xi_h, xi_l], 1)
    yi_h, yi_l = split_table(np.block([[c.T, s.T], [-s.T, c.T]]) / G)
    yi = np.concatenate([yi_h, yi_h, yi_l, yi_l], 0)
    back = np.where(kz == 0, 1.0, 2.0)[:, None] / G
    zb = zt * back[:, :, None]
    zi_h, zi_l = split_table(np.einsum("krz,cd->czkrd", zb, four).reshape(4 * G, 8 * KZ))
    zi = np.concatenate([zi_h, zi_h, zi_l], 1)
    zs_h, zs_l = split_table(np.repeat(zb.transpose(2, 0, 1), NX, axis=1).reshape(G, 2 * KZ * NX))
    zs = np.concatenate([zs_h, zs_h, zs_l], 1)
    return [jnp.asarray(t, BF16) for t in (zf, yf, xf, xi, yi, zi, zs)]


def dot(a, b):
    return jnp.dot(a, b, preferred_element_type=F32)


def split(value):
    high = value.astype(BF16)
    low = (value - high.astype(F32)).astype(BF16)
    return high, low


def swap8(tiles):
    row = lax.broadcasted_iota(jnp.int32, (8, 128), 0)
    for d in (1, 2, 4):
        mask = (row // d) % 2 == 0
        new = list(tiles)
        for i in range(8):
            if i & d:
                continue
            a, b = tiles[i], tiles[i + d]
            new[i] = jnp.where(mask, a, pltpu.roll(b, d, 0))
            new[i + d] = jnp.where(mask, pltpu.roll(a, 8 - d, 0), b)
        tiles = new
    return tiles


def split3(value):
    high = value.astype(BF16)
    rest = value - high.astype(F32)
    mid = rest.astype(BF16)
    return high, mid, (rest - mid.astype(F32)).astype(BF16)


def pick(chosen, value):
    return dot(chosen, jnp.concatenate(split3(value), axis=0))


def lanes(shape):
    return lax.broadcasted_iota(jnp.int32, shape, len(shape) - 1)


def split_lanes(value):
    high = value.astype(BF16).astype(F32)
    return jnp.where(lanes(value.shape) < 64, high, value - high).astype(BF16)


def fold(value):
    return value + pltpu.roll(value, 64, 1)


def swap16(tiles):
    group = lanes(tiles[0].shape) // 8
    for d in (1, 2, 4, 8):
        mask = (group // d) % 2 == 0
        new = list(tiles)
        for i in range(16):
            if i & d:
                continue
            a, b = tiles[i], tiles[i + d]
            new[i] = jnp.where(mask, a, pltpu.roll(b, 8 * d, 1))
            new[i + d] = jnp.where(mask, pltpu.roll(a, G - 8 * d, 1), b)
        tiles = new
    return tiles


def kernel_tiles(px, py, pz):
    def local(p):
        q = p * 0.125
        return jnp.broadcast_to(q - jnp.floor(q), (8, 128))

    ux, uy, uz = local(px), local(py), local(pz)
    centre = (lax.broadcasted_iota(jnp.int32, (8, 128), 0).astype(F32) + 0.5) * 0.125
    gap = centre - uy
    base = 1.0 - gap * gap
    ex, ez = [], []
    for a in range(8):
        gx = (a + 0.5) * 0.125 - ux
        ex.append(gx * gx)
        gz = (a + 0.5) * 0.125 - uz
        ez.append(base - gz * gz)
    out = []
    for z in range(8):
        for x in range(8):
            t = jnp.maximum(ez[z] - ex[x], 0.0)
            out.append(t * t)
    return out


def points_offset(t):
    step = lax.rem(t, 4)
    return step, lax.rem(step + t // 4, 4)


def mega(
    brick, count, feat, pos, area, sdf, gain, mix, bias, spec, readout, zf_h, yf_h, xf_h, xi_h, yi_h, zi_h, zs_h,
    out,
    zf, yf, xf, xi, yi, zi, zs,
    brickv, counts, posv, areav, sdfv, gains, mixv, biases, specv, readouts,
    vecv, vecs, mixf, mixt, wbuf, homes, placed,
    sbuf, rbuf, msend, mrecv, kst, contr, g, mixed, sdft,
    send, frecv, irecv, frecv1, jsend, jrecv, plane, sacc, srow, psend, precv,
    insem, featsem, bsem, psem, msem, osem, fsem, isem, f1sem, jsem, rsem, entered,
):
    gx = lax.axis_index("gx")
    gy = lax.axis_index("gy")
    me = gx * NY + gy
    cy, core = gx // 2, lax.rem(gx, 2)
    cz, cx = gy // 4, lax.rem(gy, 4)

    def peer(dz, dx):
        return lax.rem(cz + dz, 4) * 4 + lax.rem(cx + dx, 4)

    small = [
        (brick, brickv), (count, counts), (pos, posv), (area, areav), (readout, readouts), (mix, mixv), (bias, biases),
        (gain, gains), (spec, specv), (sdf, sdfv),
        (zf_h, zf), (yf_h, yf), (xf_h, xf), (xi_h, xi), (yi_h, yi), (zi_h, zi), (zs_h, zs),
    ]
    loads = [pltpu.make_async_copy(a, b, insem.at[i]) for i, (a, b) in enumerate(small)]
    for load in loads[:4]:
        load.start()

    barrier = pltpu.get_barrier_semaphore()
    for t in range(1, NY):
        pl.semaphore_signal(barrier, inc=1, device_id=(gx, lax.rem(gy + t, NY)), device_id_type=MESH)
    for t in range(1, NX):
        pl.semaphore_signal(barrier, inc=1, device_id=(lax.rem(gx + t, NX), gy), device_id_type=MESH)

    def load_feat(n, carry):
        pltpu.make_async_copy(
            feat.at[:, pl.ds(pl.multiple_of(n * 128, 128), 128)],
            mixed.at[:, n, :], featsem,
        ).start()
        return carry

    lax.fori_loop(0, SLOTS, load_feat, 0)
    for load in loads[4:]:
        load.start()

    sub = lax.broadcasted_iota(jnp.int32, (G, G), 0)
    lane = lanes((G, G))
    one = jnp.ones((G, G), jnp.int32)
    zero = jnp.zeros((G, G), jnp.int32)

    def total(value):
        return jnp.sum(value, axis=0, keepdims=True)

    loads[0].wait()
    loads[1].wait()
    blocks = jnp.broadcast_to(brickv[...], (G, G))
    live_blocks = counts[0]
    owner = lax.shift_right_logical(blocks, 4) & 15
    inner = (lax.shift_right_logical(blocks, 8) & 1) * 16 + (blocks & 15)
    owner_t = jnp.transpose(owner)
    ahead = (owner_t == owner) & (sub < lane) & (sub < live_blocks)
    slot = jnp.where(lane[0:1] < live_blocks, owner[0:1] * CAP + total(jnp.where(ahead, one, zero)), SLOTS)
    match = jnp.where(jnp.transpose(jnp.broadcast_to(slot, (G, G))) == lane, one, zero)
    bricks = jnp.where(total(match) > 0, total(match * jnp.transpose(inner)), 32)
    msend[...] = jnp.transpose(jnp.broadcast_to(bricks, (G, G)))
    mine = pl.ds(pl.multiple_of(gy * CAP, CAP), CAP)
    mrecv[mine, :] = msend[mine, :]
    back_home = match.astype(F32).astype(BF16)
    homes[...] = jnp.concatenate([back_home] * 3, axis=1)
    to_slot = jnp.transpose(match).astype(F32).astype(BF16)
    placed[...] = jnp.concatenate([to_slot] * 3, axis=1)

    loads[2].wait()
    loads[3].wait()
    pltpu.make_async_copy(mixed, mixed, featsem).wait()

    areas = jnp.concatenate([areav[:, 128 * n : 128 * n + 128] for n in range(SLOTS)], axis=0)
    scale = pick(placed[...], areas)

    def pack(c, carry):
        h, l = split(mixed[c])
        o = dot(placed[:, 0:256], jnp.concatenate([h, l], axis=0)) * scale
        for j in range(NY):
            sbuf[j, pl.ds(pl.multiple_of(c * CAP, CAP), CAP), :] = o[CAP * j : CAP * j + CAP]
        return carry

    lax.fori_loop(0, 32, pack, 0, unroll=2)
    for k in range(3):
        o = pick(placed[...], jnp.concatenate([posv[k : k + 1, 128 * n : 128 * n + 128] for n in range(SLOTS)], axis=0))
        for j in range(NY):
            sbuf[j, 256 + 8 * k : 264 + 8 * k, :] = o[CAP * j : CAP * j + CAP]
    pl.semaphore_wait(barrier, NY + NX - 2)

    for dz, dx in POINTS[1:]:
        j = peer(dz, dx)
        pltpu.make_async_remote_copy(
            src_ref=msend.at[pl.ds(pl.multiple_of(j * CAP, CAP), CAP), :], dst_ref=mrecv.at[mine, :],
            send_sem=msem.at[0], recv_sem=msem.at[1], device_id=(gx, j), device_id_type=MESH,
        ).start()
    for dz, dx in POINTS[1:]:
        j = peer(dz, dx)
        pltpu.make_async_remote_copy(
            src_ref=sbuf.at[j], dst_ref=rbuf.at[gy],
            send_sem=bsem, recv_sem=psem.at[gy], device_id=(gx, j), device_id_type=MESH,
        ).start()
    for t in range(1, NX):
        pl.semaphore_signal(entered, inc=1, device_id=(lax.rem(gx + t, NX), gy), device_id_type=MESH)
    rbuf[gy] = sbuf[gy]

    for load in loads[4:]:
        load.wait()
    sacc[...] = jnp.transpose(sdfv[...])
    for a in range(8):
        sdft[16 * a : 16 * a + 16, :] = sacc[pl.ds(a, 16, stride=8), :]
    vec = jnp.zeros((1, 32), F32)
    shift = jnp.float32(0.0)
    for o in range(32):
        vec = vec + readouts[o] * mixv[1, o : o + 1, :]
        shift = shift + readouts[o] * biases[1, o]
    vecv[:, 0:32] = vec
    vec_copy = pltpu.make_async_copy(vecv, vecs, osem)
    vec_copy.start()
    for k in range(4):
        mixf[:, 32 * k : 32 * k + 32] = mixv[0]
    mixt[...] = split_lanes(mixf[...])
    narrow = lanes((8, 128)) < 32
    for layer in range(2):
        pair = jnp.concatenate([specv[2 * layer], specv[2 * layer + 1]], axis=0)
        for t in range(8):
            part = pair[:, 128 * t : 128 * t + 128]
            for u in range(4):
                w = jnp.where(narrow, part if u == 0 else pltpu.roll(part, G - 32 * u, 1), 0.0)
                w = w + pltpu.roll(w, 32, 1)
                wbuf[layer * 256 + (4 * t + u) * 8 : layer * 256 + (4 * t + u) * 8 + 8, :] = w + pltpu.roll(w, 64, 1)
    vec_copy.wait()

    whole = mrecv.at[pl.ds(0, (NY - 1) * CAP), :]
    pltpu.make_async_copy(whole, whole, msem.at[0]).wait()
    pltpu.make_async_copy(whole, whole, msem.at[1]).wait()
    inside = jnp.where(jnp.transpose(mrecv[...])[0:32] == sub[0:32], 1.0, 0.0).astype(BF16)
    inside = jnp.concatenate([inside, inside], axis=1)

    def encode(t, carry):
        dz, dx = points_offset(t)
        j = lax.rem(cz + 4 - dz, 4) * 4 + lax.rem(cx + 4 - dx, 4)

        @pl.when(t > 0)
        def _():
            pltpu.make_async_copy(rbuf.at[j], rbuf.at[j], psem.at[j]).wait()

        outs = []
        for i in range(CAP):
            tiles = kernel_tiles(
                rbuf[j, 256 + i : 257 + i, :], rbuf[j, 264 + i : 265 + i, :], rbuf[j, 272 + i : 273 + i, :]
            )
            kh, kl = split(jnp.concatenate(tiles, axis=0))
            fh, fl = split(rbuf[j, pl.ds(i, 32, stride=CAP), :])
            lhs = jnp.concatenate(
                [jnp.concatenate([fh, fh], axis=1), jnp.concatenate([fl, jnp.zeros_like(fl)], axis=1)], axis=0
            )
            rhs = jnp.concatenate([kh, kl], axis=1)
            kst[j * CAP + i] = rhs
            o = lax.dot_general(lhs, rhs, (((1,), (1,)), ((), ())), preferred_element_type=F32)
            outs.append(o[0:32] + o[32:64])
        for b in range(4):
            for q in range(4):
                turned = swap8([outs[i][8 * b : 8 * b + 8, 128 * q : 128 * q + 128] for i in range(CAP)])
                for i in range(CAP):
                    row = pl.multiple_of((8 * b + i) * SLOTS + j * CAP, CAP)
                    contr[q, pl.ds(row, CAP), :] = turned[i]
        return carry

    lax.fori_loop(0, NY, encode, 0)

    low = lanes((16, 128)) < 64
    pl.semaphore_wait(entered, NX - 1)

    def group_of(t):
        u = t // 2
        dy = lax.rem(2 + 3 * u + 3 * (u // 2) + 2 * (u // 3), 4)
        return lax.rem(cy + dy, 4) * 2 + lax.rem(core + 1 + lax.rem(t, 2), 2)

    partners = [peer(dz, dx) for dz, dx in FAR]

    def issue(t, grp, source_row, recv, row, size, sem):
        for n, k in enumerate(partners):
            copy = pltpu.make_async_remote_copy(
                src_ref=send.at[pl.ds(pl.multiple_of(source_row(k), size), size), :] if size == 8
                else jsend.at[pl.ds(pl.multiple_of(source_row(k), size), size), :],
                dst_ref=recv.at[pl.ds(pl.multiple_of(row, size), size), :],
                send_sem=sem.at[0], recv_sem=sem.at[1], device_id=(grp, k), device_id_type=MESH,
            )
            if n < NY - 1:
                copy.start()
            else:
                pl.when(t < NX - 1)(copy.start)

    def forward(recv, sem, prepare):
        def group(t, carry):
            grp = group_of(t)
            h, l = split(jnp.concatenate(prepare(grp), axis=0))
            rows = pl.ds(pl.multiple_of(grp * 128, 128), 128)
            send[rows, :] = dot(zf[...], jnp.concatenate([h, l, h], axis=0))
            issue(t, grp, lambda k: (grp * NY + k) * 8, recv, me * 8, 8, sem)
            return carry

        lax.fori_loop(0, NX, group, 0)
        recv[pl.ds(pl.multiple_of(me * 8, 8), 8), :] = send[pl.ds(pl.multiple_of(me * 8, 8), 8), :]

    def arrive(recv, sem, size=8):
        part = recv.at[pl.ds(0, (NX * NY - 1) * size), :]
        pltpu.make_async_copy(part, part, sem.at[1]).wait()
        pltpu.make_async_copy(part, part, sem.at[0]).wait()

    sign_f = jnp.where(lanes((1, 128)) % 64 < 32, 1.0, -1.0)

    def modes(recv, layer):
        for a in range(NX):
            tiles = [recv[(a * 16 + b) * 8 : (a * 16 + b) * 8 + 8, :] for b in range(16)]
            tiles = swap16(tiles)
            for b in (0, 8):
                turned = swap8(tiles[b : b + 8])
                for n in range(8):
                    plane[n * G + a * 16 + b : n * G + a * 16 + b + 8, :] = turned[n]
        both = jnp.concatenate(
            [
                jnp.concatenate([plane[G * ci : G * ci + G, :], plane[G * ci + 4 * G : G * ci + 5 * G, :]], axis=1)
                for ci in range(4)
            ],
            axis=0,
        )
        h, l = split(both)
        y = fold(dot(jnp.concatenate([h, l], axis=1), yf[...]))
        y2 = pltpu.roll(y, 96, 1) * sign_f
        r = [
            jnp.concatenate([split_lanes(y[G * ci : G * ci + G]), split_lanes(y2[G * ci : G * ci + G])], axis=0)
            for ci in range(4)
        ]
        z4 = dot(xf[...], jnp.concatenate(r, axis=1))
        z4 = z4[0:32] + z4[32:64]
        result = []
        for ci in range(4):
            z = fold(z4[:, 128 * ci : 128 * ci + 128])
            wr = wbuf[pl.ds(layer * 256 + ci, M, stride=8), :]
            wi = wbuf[pl.ds(layer * 256 + 4 + ci, M, stride=8), :]
            result.append(z * wr - pltpu.roll(z, 96, 1) * (wi * sign_f))
        return result

    def inverse_planes(parts):
        r = []
        for p in parts:
            pair = jnp.concatenate([split_lanes(p), split_lanes(pltpu.roll(p, 96, 1) * (-sign_f))], axis=0)
            r.append(jnp.concatenate([pair, pair], axis=0))
        q4 = dot(xi[...], jnp.concatenate(r, axis=1))
        q = jnp.concatenate([split_lanes(fold(q4[:, 128 * n : 128 * n + 128])) for n in range(len(parts))], axis=0)
        return dot(jnp.concatenate([q, q], axis=1), yi[...])

    def prepare0(grp):
        values = []
        for ci in range(4):
            c = grp * 4 + ci
            pieces = []
            for q in range(4):
                h, l = split(contr[q, pl.ds(pl.multiple_of(c * SLOTS, SLOTS), SLOTS), :])
                o = dot(inside, jnp.concatenate([h, l], axis=0))
                a, b = o[0:16], o[16:32]
                pieces.append(jnp.where(low, a, pltpu.roll(b, 64, 1)))
                pieces.append(jnp.where(low, pltpu.roll(a, 64, 1), b))
            value = jnp.concatenate(pieces, axis=0) + gains[c] * sdft[...]
            g[pl.ds(pl.multiple_of(c * G, G), G), :] = value
            values.append(value)
        return values

    forward(frecv, fsem, prepare0)

    mixed2 = mixed.reshape(32 * G, 128)

    def mix_cells(z, carry):
        h, l = split(g[pl.ds(z, 32, stride=G), :])
        mixed2[pl.ds(z, 32, stride=G), :] = dot(mixt[...], jnp.concatenate([h, l, h, l], axis=0))
        return carry

    lax.fori_loop(0, G // 2, mix_cells, 0, unroll=4)
    arrive(frecv, fsem)
    o = inverse_planes(modes(frecv, 0))
    for ci in range(4):
        plane[G * ci : G * ci + G, :] = o[G * ci : G * ci + G, 0:128]
        plane[G * ci + 4 * G : G * ci + 5 * G, :] = o[G * ci : G * ci + G, 128:256]

    spot = gy * NX + gx

    def back(t, carry):
        grp = group_of(t)
        base = pl.multiple_of(grp * 128, 128)
        tiles = []
        for b in (0, 8):
            row = pl.multiple_of(grp * 16 + b, 8)
            tiles += swap8([plane[pl.ds(n * G + row, 8), :] for n in range(8)])
        tiles = swap16(tiles)
        for b in range(16):
            send[pl.ds(base + 8 * b, 8), :] = tiles[b]
        issue(t, grp, lambda k: (grp * NY + k) * 8, irecv, me * 8, 8, isem)
        return carry

    lax.fori_loop(0, NX, back, 0)
    irecv[pl.ds(pl.multiple_of(me * 8, 8), 8), :] = send[pl.ds(pl.multiple_of(me * 8, 8), 8), :]
    lax.fori_loop(G // 2, G, mix_cells, 0, unroll=4)
    arrive(irecv, isem)
    sacc[...] = jnp.zeros_like(sacc) + shift

    def prepare1(grp):
        h, l = split(irecv[pl.ds(pl.multiple_of(grp * 128, 128), 128), :])
        spectral = dot(zi[...], jnp.concatenate([h, l, h], axis=0))
        values = []
        added = None
        for ci in range(4):
            c = grp * 4 + ci
            value = jax.nn.gelu(spectral[G * ci : G * ci + G] + mixed[c] + biases[0, c])
            added = vecs[0, c] * value if added is None else added + vecs[0, c] * value
            values.append(value)
        sacc[...] += added
        return values

    forward(frecv1, f1sem, prepare1)
    arrive(frecv1, f1sem)
    projected = None
    for ci, p in enumerate(modes(frecv1, 1)):
        p = p * readouts[gx * 4 + ci]
        projected = p if projected is None else projected + p
    o = inverse_planes([projected])
    for a in range(NX):
        for ri in range(2):
            plane[pl.ds((a // 4) * 128 + (a % 4) * 2 + ri, 16, stride=8), :] = o[16 * a : 16 * a + 16, 128 * ri : 128 * ri + 128]
    for half in range(2):
        tiles = swap16([plane[half * 128 + 8 * b : half * 128 + 8 * b + 8, :] for b in range(16)])
        for b in range(16):
            jsend[half * 128 + 8 * b : half * 128 + 8 * b + 8, :] = tiles[b]

    def back1(t, carry):
        grp = group_of(t)
        issue(t, grp, lambda k: ((grp // 4) * 16 + k) * 8 + lax.rem(grp, 4) * 2, jrecv, spot * 2, 2, jsem)
        return carry

    lax.fori_loop(0, NX, back1, 0)
    jrecv[pl.ds(pl.multiple_of(spot * 2, 2), 2), :] = jsend[
        pl.ds(pl.multiple_of(((gx // 4) * 16 + gy) * 8 + lax.rem(gx, 4) * 2, 2), 2), :
    ]
    arrive(jrecv, jsem, 2)
    h, l = split(jrecv[...])
    field = sacc[...] + dot(zs[...], jnp.concatenate([h, l, h], axis=0))

    left = lanes((16, 128)) < 64
    for q in range(4):
        a = field[32 * q : 32 * q + 16]
        b = field[32 * q + 16 : 32 * q + 32]
        for bx in range(2):
            w = jnp.where(left, a, pltpu.roll(b, 64, 1)) if bx == 0 else jnp.where(left, pltpu.roll(a, 64, 1), b)
            h, l = split(w)
            srow[16 * bx : 16 * bx + 16, 128 * q : 128 * q + 128] = h
            srow[32 + 16 * bx : 48 + 16 * bx, 128 * q : 128 * q + 128] = l
    srow[64:80, :] = jnp.ones((16, 512), BF16)
    which = sub[0:32]

    def decode(u, carry):
        dz, dx = points_offset(NY - 1 - u)
        j = peer(dz, dx)
        nums, dens = [], []
        for i in range(CAP):
            o = dot(srow[...], kst[j * CAP + i])
            o = o[0:72, 0:128] + o[0:72, 128:256]
            owned = jnp.broadcast_to(mrecv[pl.ds(j * CAP + i, 1), :], (32, 128)) == which
            nums.append(total(jnp.where(owned, o[0:32] + o[32:64], 0.0)))
            dens.append(o[64:65])
        psend[pl.ds(pl.multiple_of(j * CAP, CAP), CAP), :] = jnp.concatenate(nums, axis=0) / jnp.concatenate(dens, axis=0)

        @pl.when(u < NY - 1)
        def _():
            pltpu.make_async_remote_copy(
                src_ref=psend.at[pl.ds(pl.multiple_of(j * CAP, CAP), CAP), :], dst_ref=precv.at[mine, :],
                send_sem=rsem.at[0], recv_sem=rsem.at[1], device_id=(gx, j), device_id_type=MESH,
            ).start()

        return carry

    lax.fori_loop(0, NY, decode, 0)
    precv[mine, :] = psend[mine, :]
    part = precv.at[pl.ds(0, (NY - 1) * CAP), :]
    pltpu.make_async_copy(part, part, rsem.at[1]).wait()
    pltpu.make_async_copy(part, part, rsem.at[0]).wait()
    sent = sbuf.at[pl.ds(0, NY - 1)]
    pltpu.make_async_copy(sent, sent, bsem).wait()

    out[...] = pick(homes[...], precv[...])


def per_device(positions, point_feat, area, block_brick, block_count, sdf, grid_gain, mix_w, mix_b, spec_w, readout_w):
    consts = tables()
    hbm = pl.BlockSpec(memory_space=pl.ANY)
    dma = pltpu.SemaphoreType.DMA
    vmem = pltpu.VMEM
    i32 = jnp.int32
    out = pl.pallas_call(
        mega,
        out_shape=jax.ShapeDtypeStruct((SLOTS, 128), F32),
        in_specs=[hbm] * (11 + len(consts)),
        out_specs=pl.BlockSpec(memory_space=vmem),
        scratch_shapes=[vmem(t.shape, BF16) for t in consts]
        + [
            vmem((1, SLOTS), i32),
            pltpu.SMEM((1,), i32),
            vmem((3, SLOTS * 128), F32),
            vmem((1, SLOTS * 128), F32),
            vmem((G, 128), F32),
            pltpu.SMEM((32,), F32),
            vmem((2, 32, 32), F32),
            pltpu.SMEM((2, 32), F32),
            vmem((4, 4, M * M), F32),
            pltpu.SMEM((32,), F32),
            vmem((1, 128), F32),
            pltpu.SMEM((1, 128), F32),
            vmem((32, 128), F32),
            vmem((32, 128), BF16),
            vmem((512, 128), F32),
            vmem((SLOTS, 384), BF16),
            vmem((SLOTS, 384), BF16),
            vmem((NY, ROWS, 128), F32),
            vmem((NY, ROWS, 128), F32),
            vmem((SLOTS, 128), i32),
            vmem((SLOTS, 128), i32),
            vmem((SLOTS, 512, 256), BF16),
            vmem((4, SLOTS * 32, 128), F32),
            vmem((32 * G, 128), F32),
            vmem((32, G, 128), F32),
            vmem((G, 128), F32),
            vmem((1024, 128), F32),
            vmem((1024, 128), F32),
            vmem((1024, 128), F32),
            vmem((1024, 128), F32),
            vmem((256, 128), F32),
            vmem((256, 128), F32),
            vmem((1024, 128), F32),
            vmem((G, 128), F32),
            vmem((80, 512), BF16),
            vmem((SLOTS, 128), F32),
            vmem((SLOTS, 128), F32),
            dma((10 + len(consts),)), dma, dma, dma((NY,)), dma((2,)), dma, dma((2,)), dma((2,)), dma((2,)),
            dma((2,)), dma((2,)), pltpu.SemaphoreType.REGULAR,
        ],
        compiler_params=pltpu.CompilerParams(collective_id=0, has_side_effects=True, vmem_limit_bytes=67043328),
        name="operator",
    )(
        block_brick.reshape(1, SLOTS), block_count, point_feat, positions, area.reshape(1, SLOTS * 128), sdf.reshape(G, 128),
        grid_gain, mix_w, mix_b, spec_w.reshape(4, 4, M * M), readout_w, *consts,
    )
    return out.reshape(SLOTS * 128)


def solution(mesh):
    placed = (
        P(None, ("gx", "gy")),
        P(None, ("gx", "gy")),
        P(("gx", "gy")),
        P(("gx", "gy")),
        P(("gx", "gy")),
        P("gx", "gy", None),
        P(),
        P(),
        P(),
        P(None, None, "gy", "gx", None),
        P(),
    )
    return jax.shard_map(per_device, mesh=mesh, in_specs=placed, out_specs=P(("gx", "gy")), check_vma=False)
```
